512 devices in a mesh: seq: 64 (over z_lo, y, core), tp: 8 (over z_hi, x).
Axes of the slice: x: 4, y: 4, z: 16 (z_hi: 2, z_lo: 8; z = z_hi * 8 + z_lo), core: 2. Of those that a mesh axis runs over, the one named last changes fastest.
Arguments:
- queries: bfloat16 [16384, 2048], P('seq', 'tp'), may hold values from -42 to 42
- keys: bfloat16 [16384, 2048], P('seq', 'tp'), may hold values from -6.1 to 6.1
- values: bfloat16 [16384, 2048], P('seq', 'tp'), may hold values from -6 to 6
- residual_in: bfloat16 [16384, 2048], P('seq', 'tp'), may hold values from -6 to 6
- bias_table: float32 [16, 32], P('tp'), may hold values from -4 to 4
- buckets: int32 [128, 33], P('seq'), may hold values from 0 to 31
- out_weight: bfloat16 [2048, 2048], P('tp'), may hold values from -0.125 to 0.125
- gate_weight: bfloat16 [2048, 4096], P('seq', 'tp'), may hold values from -0.125 to 0.125
- up_weight: bfloat16 [2048, 4096], P('seq', 'tp'), may hold values from -0.125 to 0.125
- down_weight_t: bfloat16 [2048, 4096], P('seq', 'tp'), may hold values from -0.09375 to 0.09375
- norm_gain: float32 [2048], replicated, may hold values from 0.5 to 1.5
Outputs:
- layer_out: bfloat16 [16384, 2048], P('seq', 'tp')
The draws below stay inside these ranges and needn't reach their ends.
All inputs are finite; a program needn't handle non-finite values.
Results may differ from the reference program's by a relative error of at most 0.015.
Values may be sent and summed in bfloat16 or wider, within the bound.
A program may use at most 64 MiB of HBM per device.

```python
import jax
import jax.numpy as jnp
from jax import lax

D = 2048
HEADS = 16
HEAD_DIM = 128
FF = 4096
BUCKETS = 32
TILE = 128
HALF_BAND = 2048
BINS_DEV = 256
HH = 2048
SEQ_LEN = 16384
NTILES = 128
OFFSETS = 33
N_SEQ = 64
N_TP = 8


def draw_pair(key):
    base = jax.random.fold_in(key, 4242)
    key_query, key_keys = jax.random.split(base, 2)
    shape = (SEQ_LEN, HEADS * HEAD_DIM)
    query_out = jnp.clip(jax.random.normal(key_query, shape, jnp.float32), -6.0, 6.0)
    key_out = jnp.clip(jax.random.normal(key_keys, shape, jnp.float32), -6.0, 6.0)
    return (query_out, key_out)


def draw_queries(key, part):
    return draw_pair(key)[0].astype(jnp.bfloat16)


def draw_keys(key, part):
    return draw_pair(key)[1].astype(jnp.bfloat16)


def place_ends(values, key, least, high):
    shape = values.shape
    place = [jax.random.randint(jax.random.fold_in(key, axis), (), 0, shape[axis]) for axis in range(len(shape))]
    values = values.at[tuple(place)].set(least)
    longest = shape.index(max(shape))
    place[longest] = (place[longest] + 1) % shape[longest]
    return values.at[tuple(place)].set(high)


def block_levels(stream_key, shape, shards, low, largest):
    factor_of = 1.0
    for axis_at, parts in shards:
        draws = jax.random.uniform(jax.random.fold_in(jax.random.fold_in(stream_key, 6), axis_at), (parts,), jnp.float32, low / len(shards), largest / len(shards))
        factor_of = factor_of * jnp.repeat(jnp.exp(draws), shape[axis_at] // parts).reshape((-1,) + (1,) * (len(shape) - 1 - axis_at))
    return factor_of


def normal_values(stream_key, dims, deviation, reach, shards=(), kind=jnp.bfloat16):
    drawn = deviation * jax.random.normal(stream_key, dims, jnp.float32)
    if shards:
        drawn = drawn * block_levels(stream_key, dims, shards, -0.22, 0.18)
    return jnp.clip(drawn, -reach, reach).astype(kind)


def setup_inputs(seed: int = 0) -> dict:
    splits = jax.random.split(jax.random.key(seed), 12)
    queries = draw_queries(jax.random.fold_in(splits[11], 71), 0)
    keys = draw_keys(jax.random.fold_in(splits[11], 71), 0)
    values = normal_values(splits[2], (SEQ_LEN, HH), 1.0, 6.0, ((0, 64), (1, 8)))
    residual_in = normal_values(splits[3], (SEQ_LEN, D), 1.0, 6.0, ((0, 64), (1, 8)))
    bias_table = normal_values(splits[4], (HEADS, BUCKETS), 1.0, 4.0, ((0, 8),), jnp.float32)
    buckets = place_ends(jax.random.randint(splits[5], (NTILES, OFFSETS), 0, BUCKETS), jax.random.fold_in(splits[5], 1), 0, BUCKETS - 1).astype(jnp.int32)
    out_weight = normal_values(splits[6], (HH, D), HH ** -0.5, 0.125, ((0, 8),))
    gate_weight = normal_values(splits[7], (D, FF), D ** -0.5, 0.125, ((0, 64), (1, 8)))
    up_weight = normal_values(splits[8], (D, FF), D ** -0.5, 0.125, ((0, 64), (1, 8)))
    down_weight_t = normal_values(splits[9], (D, FF), FF ** -0.5, 0.09375, ((0, 64), (1, 8)))
    norm_gain = jnp.clip(1.0 + 0.1 * jax.random.normal(splits[10], (D,), jnp.float32), 0.5, 1.5)
    return {"queries": queries, "keys": keys, "values": values, "residual_in": residual_in, "bias_table": bias_table, "buckets": buckets, "out_weight": out_weight, "gate_weight": gate_weight, "up_weight": up_weight, "down_weight_t": down_weight_t, "norm_gain": norm_gain}


def attend_block(q_blk, k_blk, v_blk, bucket_blk, bias_table, start):
    rows = q_blk.shape[0]
    width = HALF_BAND
    span = rows + 2 * width
    scores = jnp.einsum('qhd,khd->hqk', q_blk.astype(jnp.float32), k_blk.astype(jnp.float32)) * HEAD_DIM ** (-0.5)
    tiles_q = rows // TILE
    tiles_k = span // TILE
    onehot = (bucket_blk[:, :, None] == jnp.arange(BUCKETS, dtype=jnp.int32)[None, None, :]).astype(jnp.float32)
    table_vals = jnp.einsum('qob,hb->hqo', onehot, bias_table, precision=lax.Precision.HIGHEST)
    offset = jnp.arange(tiles_k, dtype=jnp.int32)[None, :] - jnp.arange(tiles_q, dtype=jnp.int32)[:, None]
    select = (offset[:, :, None] == jnp.arange(OFFSETS, dtype=jnp.int32)[None, None, :]).astype(jnp.float32)
    tile_bias = jnp.einsum('qko,hqo->hqk', select, table_vals, precision=lax.Precision.HIGHEST)
    scores = scores.reshape(HEADS, tiles_q, TILE, tiles_k, TILE) + tile_bias[:, :, None, :, None]
    scores = scores.reshape(HEADS, rows, span)
    qpos = start + jnp.arange(rows, dtype=jnp.int32)[:, None]
    kpos = start - width + jnp.arange(span, dtype=jnp.int32)[None, :]
    valid = (jnp.abs(qpos - kpos) <= width) & (kpos >= 0) & (kpos < SEQ_LEN)
    masked = jnp.where(valid[None], scores, -1e+30)
    top = lax.optimization_barrier(jnp.max(masked, axis=-1, keepdims=True))
    expo = jnp.where(valid[None], jnp.exp(masked - top), 0.0)
    weight = (expo / lax.optimization_barrier(jnp.sum(expo, axis=-1, keepdims=True))).astype(jnp.bfloat16)
    out = jnp.einsum('hqk,khd->qhd', weight.astype(jnp.float32), v_blk.astype(jnp.float32))
    return out.astype(jnp.bfloat16).reshape(rows, HH)

def reference(queries, keys, values, residual_in, bias_table, buckets, out_weight, gate_weight, up_weight, down_weight_t, norm_gain):
    width = HALF_BAND
    rows = BINS_DEV
    tiles_q = rows // TILE
    q3 = queries.reshape(SEQ_LEN, HEADS, HEAD_DIM)
    k3 = jnp.pad(keys.reshape(SEQ_LEN, HEADS, HEAD_DIM), ((width, width), (0, 0), (0, 0)))
    v3 = jnp.pad(values.reshape(SEQ_LEN, HEADS, HEAD_DIM), ((width, width), (0, 0), (0, 0)))

    def block(index):
        start = (index * rows).astype(jnp.int32)
        q_blk = lax.dynamic_slice_in_dim(q3, start, rows, 0)
        k_blk = lax.dynamic_slice_in_dim(k3, start, rows + 2 * width, 0)
        v_blk = lax.dynamic_slice_in_dim(v3, start, rows + 2 * width, 0)
        bucket_blk = lax.dynamic_slice_in_dim(buckets, (index * tiles_q).astype(jnp.int32), tiles_q, 0)
        return attend_block(q_blk, k_blk, v_blk, bucket_blk, bias_table, start)
    attended = lax.map(block, jnp.arange(N_SEQ, dtype=jnp.int32)).reshape(SEQ_LEN, HH)
    proj = jnp.dot(attended, out_weight, preferred_element_type=jnp.float32)
    state = (residual_in.astype(jnp.float32) + proj).astype(jnp.bfloat16)
    part_width = FF // N_TP

    def feed(state_blk):
        wide = state_blk.astype(jnp.float32)
        scale = lax.rsqrt(lax.optimization_barrier(jnp.mean(wide * wide, axis=-1, keepdims=True)) + 1e-05)
        normed = (wide * scale * norm_gain.astype(jnp.float32)).astype(jnp.bfloat16)
        gate = jnp.dot(normed, gate_weight, preferred_element_type=jnp.float32)
        up = jnp.dot(normed, up_weight, preferred_element_type=jnp.float32)
        hidden = (jax.nn.silu(gate) * up).astype(jnp.bfloat16)
        total = jnp.zeros(wide.shape, jnp.float32)
        for block_id in range(N_TP):
            lo = block_id * part_width
            part = lax.dot_general(hidden[:, lo:lo + part_width], down_weight_t[:, lo:lo + part_width], (((1,), (1,)), ((), ())), preferred_element_type=jnp.float32)
            part = lax.optimization_barrier(part.astype(jnp.bfloat16))
            total = total + part.astype(jnp.float32)
        return (wide + total).astype(jnp.bfloat16)
    blocks = state.reshape(N_SEQ, BINS_DEV, D)
    return lax.map(feed, blocks).reshape(SEQ_LEN, D)
```

```python
import jax
import jax.numpy as jnp
from jax import lax
from jax.experimental import pallas as pl
from jax.experimental.pallas import tpu as pltpu
from jax.sharding import PartitionSpec as P

HEAD_DIM = 128
TILE = 128
HALF_BAND = 2048
OFFSETS = 33
NZ = 8
NY = 4
NX = 4
CHIPS = NZ * NY
ROWS = 256
COLS = 256
FFB = 512
WROWS = 32
SCALE = HEAD_DIM ** (-0.5)
MESH = pl.DeviceIdType.MESH
F32 = jnp.float32
BF16 = jnp.bfloat16


def remote(src, dst, send_sem, recv_sem, dev):
    return pltpu.make_async_remote_copy(
        src_ref=src,
        dst_ref=dst,
        send_sem=send_sem,
        recv_sem=recv_sem,
        device_id=dev,
        device_id_type=MESH,
    )


class Place:
    def __init__(self):
        s = lax.axis_index("seq")
        t = lax.axis_index("tp")
        self.s, self.t = s, t
        self.c = lax.rem(s, 2)
        self.chip = s // 2
        self.y = lax.rem(self.chip, NY)
        self.z = self.chip // NY
        self.x = lax.rem(t, NX)
        self.h = t // NX
        self.sib = (s + 1 - 2 * self.c, t)
        self.yp = lax.rem(self.y + 1, NY)
        self.ym = lax.rem(self.y + 3, NY)
        self.y2 = lax.rem(self.y + 2, NY)
        self.dyp = self.dev(self.z, self.yp)
        self.dym = self.dev(self.z, self.ym)
        self.dy2 = self.dev(self.z, self.y2)
        self.dzp = self.dev(self.z + 1, self.y)
        self.dzm = self.dev(self.z - 1, self.y)
        self.dx = [None] + [(s, self.h * NX + lax.rem(self.x + d, NX)) for d in (1, 2, 3)]
        self.far = (s, (1 - self.h) * NX + self.x)
        zz = self.h * NZ + self.z
        self.dq = []
        for step in (4, 12):
            zq = lax.rem(zz + step, 2 * NZ)
            seq = ((lax.rem(zq, NZ)) * NY + self.y) * 2 + self.c
            self.dq.append((seq, (zq // NZ) * NX + self.x))

    def dev(self, z, y):
        return ((z * NY + y) * 2 + self.c, self.t)


class Gather:
    def __init__(self, at, buf, half, rs, rb, zs, ys, bs):
        self.at, self.buf, self.half = at, buf, half
        self.rs, self.rb, self.zs, self.ys, self.bs = rs, rb, zs, ys, bs

    def full(self, chip, sem, core, send_sem, dev):
        slot = self.buf.at[chip * 2 + core]
        return remote(slot, slot, send_sem, sem, dev)

    def part(self, chip, i, send_sem, dev):
        slot = self.buf.at[chip * 2 + self.at.c, pl.ds(i * self.half, self.half)]
        return remote(slot, slot, send_sem, self.rs.at[chip, i], dev)

    def sib(self, chip):
        return self.full(chip, self.rb.at[chip], self.at.c, self.bs.at[chip], self.at.sib)

    def zstep(self, k, go=True):
        at = self.at
        for way, origin, nxt, dev in (
            (0, at.z - k, at.z + 1, at.dzp),
            (1, at.z + k, at.z - 1, at.dzm),
        ):
            chip = origin * NY + at.y
            valid = jnp.logical_and(origin >= 0, origin < NZ)
            d = self.full(chip, self.rs.at[chip, 0], at.c, self.zs.at[chip, way], dev)

            @pl.when(valid)
            def _(d=d, nxt=nxt):
                if go and not (isinstance(k, int) and k == 0):
                    d.wait_recv()

                @pl.when(jnp.logical_and(nxt >= 0, nxt < NZ))
                def _():
                    if go:
                        d.start()
                    else:
                        d.wait_send()

    def each(self, k, f):
        at = self.at

        @pl.when(at.z - k >= 0)
        def _():
            f(at.z - k)

        @pl.when(jnp.logical_and(k > 0, at.z + k < NZ))
        def _():
            f(at.z + k)

    def ysend(self, k, go=True):
        at = self.at

        def f(zo):
            chip = zo * NY + at.y
            for i, dev in ((0, at.dyp), (1, at.dym)):
                d = self.full(chip, self.rs.at[chip, 0], at.c, self.ys.at[chip, i], dev)
                d.start() if go else d.wait_send()
            d = self.sib(chip)
            d.start() if go else d.wait_send()

        self.each(k, f)

    def yrecv(self, k, go=True):
        at = self.at

        def f(zo):
            for i, yo, dev in ((0, at.ym, at.dyp), (1, at.yp, at.dym)):
                chip = zo * NY + yo
                if go:
                    self.full(chip, self.rs.at[chip, 0], at.c, self.bs.at[chip], at.sib).wait_recv()
                r = self.part(chip, i, self.ys.at[chip, i], dev)
                d = self.sib(chip)
                if go:
                    r.start()
                    d.start()
                else:
                    r.wait_send()
                    d.wait_send()
            chip = zo * NY + at.y2
            d = self.sib(chip)
            if go:
                for i in (0, 1):
                    self.part(chip, i, self.bs.at[chip], at.sib).wait_recv()
                d.start()
            else:
                d.wait_send()

        self.each(k, f)

    def wait_other_core(self):
        at = self.at

        @pl.loop(0, CHIPS)
        def _(chip):
            self.full(chip, self.rb.at[chip], 1 - at.c, self.bs.at[chip], at.sib).wait_recv()


class Cross:
    def __init__(self, at, src, rel, dst, s1, r1, s2, r2):
        self.at = at
        self.first = [remote(src[i], rel[i], s1.at[i], r1.at[i], at.dq[i]) for i in (0, 1)]
        self.second = [remote(rel[i], dst[i], s2.at[i], r2.at[i], at.dq[i]) for i in (0, 1)]

    def send(self, i):
        self.first[i].start()

    def relay(self):
        for i in (0, 1):
            self.first[i].wait_recv()
            self.second[i].start()

    def wait(self):
        for i in (0, 1):
            self.second[i].wait_recv()

    def drain(self):
        for i in (0, 1):
            self.first[i].wait_send()
            self.second[i].wait_send()


def kernel(
    q_ref, res_ref, tab_ref, bk_ref, gain_ref, k_hbm, v_hbm, wo_hbm, g_hbm, u_hbm, d_hbm,
    out_ref,
    kvb, wbuf, wob, wo_own, att_own, att_rel, att_oth, res_rel, res_oth,
    m_ref, l_ref, acc_ref, part_ref, rs_s, rs_r, rs2_s, rs2_r, st_ref, fin_s, fin_rel, fin_r,
    keep_ref,
    loc, kv_r, kv_b, kv_s, kv_s2, kv_bs,
    w_rs, w_rb, w_zs, w_ys, w_bs, o_rs, o_rb, o_zs, o_ys, o_bs, o_far,
    x1_s, x1_r, x2_s, x2_r, x3_s, x3_r, ca, cr, cf,
):
    at = Place()
    s, c, x, h, y, z = at.s, at.c, at.x, at.h, at.y, at.z

    loads = [
        pltpu.make_async_copy(k_hbm, kvb.at[4, c, 0], loc.at[0]),
        pltpu.make_async_copy(v_hbm, kvb.at[4, c, 1], loc.at[1]),
        pltpu.make_async_copy(g_hbm, wbuf.at[s, pl.ds(0, WROWS)], loc.at[2]),
        pltpu.make_async_copy(u_hbm, wbuf.at[s, pl.ds(WROWS, WROWS)], loc.at[3]),
        pltpu.make_async_copy(d_hbm, wbuf.at[s, pl.ds(2 * WROWS, WROWS)], loc.at[4]),
        pltpu.make_async_copy(wo_hbm, wo_own, loc.at[5]),
    ]
    for d in loads:
        d.start()

    barrier = pltpu.get_barrier_semaphore()
    peers = [at.sib, at.dyp, at.dym, at.dy2, at.far] + at.dx[1:] + at.dq
    for dev in peers:
        pl.semaphore_signal(barrier, inc=1, device_id=dev, device_id_type=MESH)

    @pl.when(z < NZ - 1)
    def _():
        pl.semaphore_signal(barrier, inc=1, device_id=at.dzp, device_id_type=MESH)

    @pl.when(z > 0)
    def _():
        pl.semaphore_signal(barrier, inc=1, device_id=at.dzm, device_id_type=MESH)

    pl.semaphore_wait(barrier, len(peers) + (1 - (z + 1) // NZ) + (z + NZ - 1) // NZ)
    loads[0].wait()
    loads[1].wait()

    top = (y + 1) // 4
    low = 1 - (y + 3) // 4
    upper = y // 2
    lp, lm, l2 = 1 - 4 * top, 4 * low - 1, 2 - 4 * upper

    def kv_copy(o, to, send_sem, dev):
        return remote(kvb.at[o + 4, c], kvb.at[to + 4, c], send_sem, kv_r.at[to + 4], dev)

    def kv_sib(o):
        return remote(kvb.at[o + 4, c], kvb.at[o + 4, c], kv_bs.at[o + 4], kv_b.at[o + 4], at.sib)

    kz = [(kv_copy(0, -4, kv_s.at[0], at.dzp), z < NZ - 1), (kv_copy(0, 4, kv_s.at[1], at.dzm), z > 0)]
    ky = [
        kv_copy(0, -lp, kv_s.at[2], at.dyp),
        kv_copy(0, -lm, kv_s.at[3], at.dym),
        kv_copy(0, -l2, kv_s.at[4], at.dy2),
    ]
    for d, ok in kz:
        pl.when(ok)(d.start)
    for d in ky:
        d.start()
    kv_sib(0).start()

    cross_r = Cross(
        at,
        [res_ref.at[pl.ds(128 * i, 128)] for i in (0, 1)],
        [res_rel.at[i] for i in (0, 1)],
        [res_oth.at[pl.ds(128 * i, 128)] for i in (0, 1)],
        *[cr.at[i] for i in range(4)],
    )
    cross_r.send(0)
    cross_r.send(1)
    piece = []
    for i in (0, 1):
        rows = pl.ds(pl.multiple_of(16 * (s // 4), 16), 16)
        cols = pl.ds(pl.multiple_of(1024 * i + 256 * lax.rem(s, 4), 256), 256)
        piece.append(remote(wo_hbm.at[rows, cols], wob.at[s, i], o_far.at[0, i], o_far.at[1, i], at.far))
    for d in piece:
        d.start()

    gw = Gather(at, wbuf, 48, w_rs, w_rb, w_zs, w_ys, w_bs)
    go = Gather(at, wob, 1, o_rs, o_rb, o_zs, o_ys, o_bs)

    m_ref[...] = jnp.full(m_ref.shape, -1e30, F32)
    l_ref[...] = jnp.zeros(l_ref.shape, F32)
    acc_ref[...] = jnp.zeros(acc_ref.shape, F32)

    def update(i, sc, v):
        m_old = m_ref[i]
        m_new = jnp.maximum(m_old, jnp.max(sc, axis=1, keepdims=True))
        alpha = jnp.exp(m_old - m_new)
        p = jnp.exp(sc - m_new[:, 0:1])
        l_ref[i] = alpha * l_ref[i] + jnp.sum(p, axis=1, keepdims=True)
        pv = jnp.dot(p.astype(BF16), v, preferred_element_type=F32)
        acc_ref[i] = alpha * acc_ref[i] + pv
        m_ref[i] = m_new

    def bias_of(i, first, kt):
        idx = first + kt - lax.rem(i, 2) + HALF_BAND // TILE
        idx = jnp.clip(idx, 0, OFFSETS - 1)
        return tab_ref[i // 2, bk_ref[lax.rem(i, 2), idx]]

    def attend(o, core=None):
        @pl.loop(0, 4)
        def _(i):
            head = pl.ds(pl.multiple_of(128 * (i // 2), 128), 128)
            q = q_ref[pl.ds(pl.multiple_of(128 * lax.rem(i, 2), 128), 128), head]
            if core is None:
                n = 512
                k = kvb[o + 4, :, 0, :, head].reshape(n, 128)
                v = kvb[o + 4, :, 1, :, head].reshape(n, 128)
                first = 4 * o - 2 * c
            else:
                n = 256
                k = kvb[o + 4, core, 0, :, head]
                v = kvb[o + 4, core, 1, :, head]
                first = 4 * o + 2 * core - 2 * c
            sc = lax.dot_general(q, k, (((1,), (1,)), ((), ())), preferred_element_type=F32)
            sc = jnp.concatenate(
                [sc[:, 128 * kt : 128 * kt + 128] * SCALE + bias_of(i, first, kt) for kt in range(n // 128)],
                axis=1,
            )
            if core is not None:
                row = lax.broadcasted_iota(jnp.int32, sc.shape, 0)
                col = lax.broadcasted_iota(jnp.int32, sc.shape, 1)
                dist = col - row + (first - lax.rem(i, 2)) * TILE
                sc = jnp.where(jnp.abs(dist) <= HALF_BAND, sc, -1e30)
            update(i, sc, v)

    def inside(o):
        return jnp.logical_and(at.chip + o >= 0, at.chip + o < CHIPS)

    def got_own(o):
        kv_copy(o, o, kv_bs.at[0], at.sib).wait_recv()

    def got_sib(o):
        d = remote(kvb.at[o + 4, 1 - c], kvb.at[o + 4, 1 - c], kv_bs.at[o + 4], kv_b.at[o + 4], at.sib)
        d.wait_recv()

    for d in loads[2:5]:
        d.wait()
    gw.zstep(0)
    got_sib(0)
    attend(0)

    second = []
    for i, (delta, sgn, dev) in enumerate(
        ((lp, 1 - 2 * top, at.dyp), (lm, 2 * low - 1, at.dym), (l2, 1 - 2 * upper, at.dy2))
    ):
        src = 4 * sgn
        second.append((kv_copy(src, src - delta, kv_s2.at[i], dev), inside(src)))
    for o in (-4, 4):
        pl.when(inside(o))(lambda o=o: got_own(o))
    for d, ok in second:
        pl.when(ok)(d.start)
    for o, keep in ((-4, 1), (4, 0)):
        pl.when(jnp.logical_and(inside(o), c == keep))(lambda o=o: kv_sib(o).start())
    gw.zstep(1)
    cross_r.relay()
    for i in (0, 1):
        piece[i].wait_recv()
    go.zstep(0)
    go.ysend(0)
    for o, core in ((-4, 0), (-4, 1), (4, 0), (4, 1)):
        need = inside(o)
        if (o, core) == (-4, 0):
            need = jnp.logical_and(need, c == 0)
        if (o, core) == (4, 1):
            need = jnp.logical_and(need, c == 1)

        @pl.when(need)
        def _(o=o, core=core):
            @pl.when(c != core)
            def _():
                got_sib(o)

            attend(o, core)

    wave1 = [4 * low - 1, 1 - 4 * top, 2 - 4 * upper]
    wave2 = [2 - wave1[0], -2 - wave1[1], -wave1[2]]
    for o in wave1:
        got_own(o)
        kv_sib(o).start()
    gw.zstep(2)
    go.zstep(1)
    for n, o in enumerate(wave1):
        got_sib(o)
        attend(o)
        go.zstep(2 + n)
        if n == 1:
            gw.zstep(3)
    for o in wave2:

        @pl.when(inside(o))
        def _(o=o):
            got_own(o)
            kv_sib(o).start()

    gw.zstep(4)
    for n, o in enumerate(wave2):

        @pl.when(inside(o))
        def _(o=o):
            got_sib(o)
            attend(o)

        go.zstep(5 + n)

    for i in range(4):
        hd, a = i // 2, i % 2
        att_own[hd, pl.ds(128 * a, 128), :] = (acc_ref[i] / l_ref[i]).astype(BF16)
    cross_a = Cross(
        at,
        [att_own.at[i] for i in (0, 1)],
        [att_rel.at[i] for i in (0, 1)],
        [att_oth.at[i] for i in (0, 1)],
        *[ca.at[i] for i in range(4)],
    )
    cross_a.send(0)
    cross_a.send(1)

    @pl.loop(1, NZ)
    def _(k):
        go.ysend(k)

    gw.ysend(0)
    loads[5].wait()
    att = jnp.concatenate([att_own[0], att_own[1]], axis=1)
    order = (2, 1, 3, 0)

    def colsof(d, i):
        xd = lax.rem(x + d, NX)
        return pl.ds(pl.multiple_of(1024 * i + 256 * xd, 256), 256)

    @pl.loop(0, 4)
    def _(d):
        for i in (0, 1):
            part_ref[d, :, pl.ds(256 * i, 256)] = jnp.dot(att, wo_own[:, colsof(d, i)], preferred_element_type=F32)

    @pl.loop(0, NZ)
    def _(k):
        go.yrecv(k)

    cross_a.relay()
    gw.zstep(5)
    go.wait_other_core()
    gw.zstep(6)
    gw.zstep(7)

    @pl.loop(1, NZ)
    def _(k):
        gw.ysend(k)

    cross_a.wait()
    oth = jnp.concatenate([att_oth[0], att_oth[1]], axis=1)
    wob4 = wob.reshape(16, 4, 2, 16, 256)
    rs = [remote(rs_s.at[d - 1], rs_r.at[d - 1], x1_s.at[d - 1], x1_r.at[d - 1], at.dx[d]) for d in (1, 2, 3)]
    for d in order:
        xd = lax.rem(x + d, NX)
        for i in (0, 1):
            w = wob4[:, xd, i].reshape(256, 256)
            cols = pl.ds(256 * i, 256)
            p = part_ref[d, :, cols] + jnp.dot(oth, w, preferred_element_type=F32)
            if d:
                rs_s[d - 1, :, cols] = p.astype(BF16)
            else:
                part_ref[0, :, cols] = p
        if d:
            rs[d - 1].start()

    cross_r.wait()
    for d in rs:
        d.wait_recv()
    own = h == 0
    res0, res1 = res_ref[...].astype(F32), res_oth[...].astype(F32)
    for i in (0, 1):
        cols = pl.ds(256 * i, 256)
        r = jnp.where(own, res0, res1) if i == 0 else jnp.where(own, res1, res0)
        tot = part_ref[0, :, cols] + r
        for d in (1, 2, 3):
            tot += rs_r[d - 1, :, cols].astype(F32)
        st_ref[x, :, cols] = tot.astype(BF16)
    ag = [remote(st_ref.at[x], st_ref.at[x], x2_s.at[d - 1], x2_r.at[d - 1], at.dx[d]) for d in (1, 2, 3)]
    for d in (2, 1, 3):
        ag[d - 1].start()

    @pl.loop(0, NZ)
    def _(k):
        gw.yrecv(k)

    gw.wait_other_core()
    for d in (1, 2, 3):
        xo = lax.rem(x + 4 - d, NX)
        remote(st_ref.at[xo], st_ref.at[xo], x2_s.at[d - 1], x2_r.at[d - 1], at.dx[d]).wait_recv()

    ssq = jnp.zeros((ROWS, 1), F32)
    for xo in range(NX):
        w = st_ref[xo].astype(F32)
        ssq += jnp.sum(w * w, axis=1, keepdims=True)
    scale = lax.rsqrt(ssq / 2048.0 + 1e-05)
    gate = jnp.zeros((ROWS, FFB), F32)
    up = jnp.zeros((ROWS, FFB), F32)
    for b in range(8):
        hb, xb = b // 4, b % 4
        blk = st_ref[xb, :, 256 * hb : 256 * hb + 256].astype(F32)
        nb = (blk * scale * gain_ref[:, 256 * b : 256 * b + 256]).astype(BF16)
        gate += jnp.dot(nb, wbuf[8 * b : 8 * b + 8, 0:WROWS, :].reshape(256, FFB), preferred_element_type=F32)
        up += jnp.dot(nb, wbuf[8 * b : 8 * b + 8, WROWS : 2 * WROWS, :].reshape(256, FFB), preferred_element_type=F32)
    hidden = (gate / (1.0 + jnp.exp(-gate)) * up).astype(BF16)

    rs2 = [remote(rs2_s.at[d - 1], rs2_r.at[d - 1], x3_s.at[d - 1], x3_r.at[d - 1], at.dx[d]) for d in (1, 2, 3)]
    for d in order:
        xd = lax.rem(x + d, NX)
        for i in (0, 1):
            w = wbuf[pl.ds(8 * (4 * i + xd), 8), 2 * WROWS : 3 * WROWS, :].reshape(256, FFB)
            p = lax.dot_general(hidden, w, (((1,), (1,)), ((), ())), preferred_element_type=F32)
            cols = pl.ds(256 * i, 256)
            if d:
                rs2_s[d - 1, :, cols] = p.astype(BF16)
            else:
                part_ref[0, :, cols] = p
        if d:
            rs2[d - 1].start()
    for d in rs2:
        d.wait_recv()
    mine = pl.ds(pl.multiple_of(256 * h, 256), 256)
    theirs = pl.ds(pl.multiple_of(256 * (1 - h), 256), 256)

    def total(cols):
        tot = part_ref[0, :, cols]
        for d in (1, 2, 3):
            tot += rs2_r[d - 1, :, cols].astype(F32)
        return tot

    out_part = total(theirs).astype(BF16)
    cross_f = Cross(
        at,
        [fin_s.at[i] for i in (0, 1)],
        [fin_rel.at[i] for i in (0, 1)],
        [fin_r.at[i] for i in (0, 1)],
        *[cf.at[i] for i in range(4)],
    )
    for i in (0, 1):
        fin_s[i] = out_part[128 * i : 128 * i + 128]
        cross_f.send(i)
    keep_ref[...] = total(mine) + st_ref[x, :, mine].astype(F32)
    cross_f.relay()

    for d, ok in kz + second:
        pl.when(ok)(d.wait_send)
    for d in ky + piece + rs + ag + rs2:
        d.wait_send()
    kv_sib(0).wait_send()
    for o in wave1:
        kv_sib(o).wait_send()
    for o in wave2:
        pl.when(inside(o))(lambda o=o: kv_sib(o).wait_send())
    for o, keep in ((-4, 1), (4, 0)):
        pl.when(jnp.logical_and(inside(o), c == keep))(lambda o=o: kv_sib(o).wait_send())

    @pl.loop(0, NZ)
    def _(k):
        for g in (gw, go):
            g.zstep(k, go=False)
            g.ysend(k, go=False)
            g.yrecv(k, go=False)

    cross_r.drain()
    cross_a.drain()
    cross_f.wait()
    for i in (0, 1):
        rows = pl.ds(128 * i, 128)
        out_ref[rows, :] = (keep_ref[rows, :] + fin_r[i].astype(F32)).astype(BF16)
    cross_f.drain()


def shards(queries, keys, values, residual_in, bias_table, buckets, out_weight, gate_weight, up_weight, down_weight_t, norm_gain):
    vmem = pl.BlockSpec(memory_space=pltpu.VMEM)
    smem = pl.BlockSpec(memory_space=pltpu.SMEM)
    hbm = pl.BlockSpec(memory_space=pl.ANY)
    dma = pltpu.SemaphoreType.DMA
    v = pltpu.VMEM
    gather_sems = [dma((CHIPS, 2)), dma((CHIPS,)), dma((CHIPS, 2)), dma((CHIPS, 2)), dma((CHIPS,))]
    scratch = [
        v((9, 2, 2, ROWS, COLS), BF16),
        v((64, 96, FFB), BF16),
        v((64, 2, 16, 256), BF16),
        v((256, 2048), BF16),
        v((2, ROWS, 128), BF16),
        v((2, ROWS, 128), BF16),
        v((2, ROWS, 128), BF16),
        v((2, 128, COLS), BF16),
        v((ROWS, COLS), BF16),
        v((4, 128, 128), F32),
        v((4, 128, 128), F32),
        v((4, 128, 128), F32),
        v((4, ROWS, 512), F32),
        v((3, ROWS, 512), BF16),
        v((3, ROWS, 512), BF16),
        v((3, ROWS, 512), BF16),
        v((3, ROWS, 512), BF16),
        v((NX, ROWS, 512), BF16),
        v((2, 128, COLS), BF16),
        v((2, 128, COLS), BF16),
        v((2, 128, COLS), BF16),
        v((ROWS, COLS), F32),
        dma((6,)), dma((9,)), dma((9,)), dma((5,)), dma((3,)), dma((9,)),
        *gather_sems,
        *gather_sems,
        dma((2, 2)),
        dma((3,)), dma((3,)), dma((3,)), dma((3,)), dma((3,)), dma((3,)),
        dma((4, 2)), dma((4, 2)), dma((4, 2)),
    ]
    return pl.pallas_call(
        kernel,
        out_shape=jax.ShapeDtypeStruct((ROWS, COLS), BF16),
        in_specs=[vmem, vmem, smem, smem, vmem] + [hbm] * 6,
        out_specs=vmem,
        scratch_shapes=scratch,
        compiler_params=pltpu.CompilerParams(
            collective_id=0, has_side_effects=True, vmem_limit_bytes=60 * 1024 * 1024
        ),
        name="layer",
    )(
        queries, residual_in, bias_table, buckets, norm_gain.reshape(1, -1),
        keys, values, out_weight, gate_weight, up_weight, down_weight_t,
    )


def solution(mesh):
    return jax.shard_map(
        shards,
        mesh=mesh,
        in_specs=(
            P("seq", "tp"),
            P("seq", "tp"),
            P("seq", "tp"),
            P("seq", "tp"),
            P("tp", None),
            P("seq", None),
            P("tp", None),
            P("seq", "tp"),
            P("seq", "tp"),
            P("seq", "tp"),
            P(),
        ),
        out_specs=P("seq", "tp"),
        check_vma=False,
    )
```

```python
import jax
import jax.numpy as jnp
from jax import lax
from jax.experimental import pallas as pl
from jax.experimental.pallas import tpu as pltpu
from jax.sharding import PartitionSpec as P

HEAD_DIM = 128
TILE = 128
HALF_BAND = 2048
OFFSETS = 33
NZ = 8
NY = 4
NX = 4
CHIPS = NZ * NY
ROWS = 256
COLS = 256
FFB = 512
WROWS = 32
SCALE = HEAD_DIM ** (-0.5)
LOG2E = 1.4426950408889634
MESH = pl.DeviceIdType.MESH
F32 = jnp.float32
BF16 = jnp.bfloat16


def remote(src, dst, send_sem, recv_sem, dev):
    return pltpu.make_async_remote_copy(
        src_ref=src,
        dst_ref=dst,
        send_sem=send_sem,
        recv_sem=recv_sem,
        device_id=dev,
        device_id_type=MESH,
    )


class Place:
    def __init__(self):
        s = lax.axis_index("seq")
        t = lax.axis_index("tp")
        self.s, self.t = s, t
        self.c = lax.rem(s, 2)
        self.chip = s // 2
        self.y = lax.rem(self.chip, NY)
        self.z = self.chip // NY
        self.x = lax.rem(t, NX)
        self.h = t // NX
        self.sib = (s + 1 - 2 * self.c, t)
        self.yp = lax.rem(self.y + 1, NY)
        self.ym = lax.rem(self.y + 3, NY)
        self.y2 = lax.rem(self.y + 2, NY)
        self.dyp = self.dev(self.z, self.yp)
        self.dym = self.dev(self.z, self.ym)
        self.dy2 = self.dev(self.z, self.y2)
        self.dzp = self.dev(self.z + 1, self.y)
        self.dzm = self.dev(self.z - 1, self.y)
        self.dx = [None] + [(s, self.h * NX + lax.rem(self.x + d, NX)) for d in (1, 2, 3)]
        self.far = (s, (1 - self.h) * NX + self.x)

    def dev(self, z, y):
        return ((z * NY + y) * 2 + self.c, self.t)


class Gather:
    def __init__(self, at, buf, half, rs, rb, zs, ys, bs):
        self.at, self.buf, self.half = at, buf, half
        self.rs, self.rb, self.zs, self.ys, self.bs = rs, rb, zs, ys, bs

    def full(self, chip, sem, core, send_sem, dev):
        slot = self.buf.at[chip * 2 + core]
        return remote(slot, slot, send_sem, sem, dev)

    def part(self, chip, i, send_sem, dev):
        slot = self.buf.at[chip * 2 + self.at.c, pl.ds(i * self.half, self.half)]
        return remote(slot, slot, send_sem, self.rs.at[chip, i], dev)

    def sib(self, chip):
        return self.full(chip, self.rb.at[chip], self.at.c, self.bs.at[chip], self.at.sib)

    def zstep(self, k, go=True):
        at = self.at
        for way, origin, nxt, dev in (
            (0, at.z - k, at.z + 1, at.dzp),
            (1, at.z + k, at.z - 1, at.dzm),
        ):
            chip = origin * NY + at.y
            valid = jnp.logical_and(origin >= 0, origin < NZ)
            d = self.full(chip, self.rs.at[chip, 0], at.c, self.zs.at[chip, way], dev)

            @pl.when(valid)
            def _(d=d, nxt=nxt):
                if go and not (isinstance(k, int) and k == 0):
                    d.wait_recv()

                @pl.when(jnp.logical_and(nxt >= 0, nxt < NZ))
                def _():
                    if go:
                        d.start()
                    else:
                        d.wait_send()

    def each(self, k, f):
        at = self.at

        @pl.when(at.z - k >= 0)
        def _():
            f(at.z - k)

        @pl.when(jnp.logical_and(k > 0, at.z + k < NZ))
        def _():
            f(at.z + k)

    def ysend(self, k, go=True):
        at = self.at

        def f(zo):
            chip = zo * NY + at.y
            ways = [at.dyp, at.dym] if self.half else [at.dyp, at.dym, at.dy2]
            for i, dev in enumerate(ways):
                d = self.full(chip, self.rs.at[chip, 0], at.c, self.ys.at[chip, i], dev)
                d.start() if go else d.wait_send()
            d = self.sib(chip)
            d.start() if go else d.wait_send()

        self.each(k, f)

    def yrecv1(self, k, go=True):
        at = self.at

        def f(zo):
            for i, yo, dev in ((0, at.ym, at.dyp), (1, at.yp, at.dym)):
                chip = zo * NY + yo
                d = self.sib(chip)
                if go:
                    self.full(chip, self.rs.at[chip, 0], at.c, self.bs.at[chip], at.sib).wait_recv()
                if self.half:
                    r = self.part(chip, i, self.ys.at[chip, i], dev)
                    r.start() if go else r.wait_send()
                d.start() if go else d.wait_send()

        self.each(k, f)

    def yrecv2(self, k, go=True):
        at = self.at

        def f(zo):
            chip = zo * NY + at.y2
            d = self.sib(chip)
            if go:
                if self.half:
                    for i in (0, 1):
                        self.part(chip, i, self.bs.at[chip], at.sib).wait_recv()
                else:
                    self.full(chip, self.rs.at[chip, 0], at.c, self.bs.at[chip], at.sib).wait_recv()
                d.start()
            else:
                d.wait_send()

        self.each(k, f)

    def wait_other_core(self):
        at = self.at

        @pl.loop(0, CHIPS)
        def _(chip):
            self.full(chip, self.rb.at[chip], 1 - at.c, self.bs.at[chip], at.sib).wait_recv()


def kernel(
    q_ref, res_ref, tab_ref, bk_ref, gain_ref, k_hbm, v_hbm, wo_hbm, g_hbm, u_hbm, d_hbm,
    out_ref,
    kvb, wbuf, wob, wo_own, att_own, att_oth, res_oth,
    m_ref, l_ref, acc_ref, part_ref, rs_s, rs_r, rs2_s, rs2_r, st_ref, fin_s, fin_r, keep_ref,
    loc, kv_r, kv_b, kv_s, kv_s2, kv_bs,
    w_rs, w_rb, w_zs, w_ys, w_bs, o_rs, o_rb, o_zs, o_ys, o_bs, o_far,
    x1_s, x1_r, x2_s, x2_r, x3_s, x3_r, ca, cr, cf,
):
    at = Place()
    s, c, x, h, y, z = at.s, at.c, at.x, at.h, at.y, at.z

    loads = [
        pltpu.make_async_copy(k_hbm, kvb.at[4, c, 0], loc.at[0]),
        pltpu.make_async_copy(v_hbm, kvb.at[4, c, 1], loc.at[1]),
        pltpu.make_async_copy(g_hbm, wbuf.at[s, pl.ds(0, WROWS)], loc.at[2]),
        pltpu.make_async_copy(u_hbm, wbuf.at[s, pl.ds(WROWS, WROWS)], loc.at[3]),
        pltpu.make_async_copy(d_hbm, wbuf.at[s, pl.ds(2 * WROWS, WROWS)], loc.at[4]),
        pltpu.make_async_copy(wo_hbm, wo_own, loc.at[5]),
    ]
    for d in loads:
        d.start()

    barrier = pltpu.get_barrier_semaphore()
    peers = [at.far] + at.dx[1:] + [at.sib, at.dyp, at.dym, at.dy2]
    for dev in peers:
        pl.semaphore_signal(barrier, inc=1, device_id=dev, device_id_type=MESH)

    @pl.when(z < NZ - 1)
    def _():
        pl.semaphore_signal(barrier, inc=1, device_id=at.dzp, device_id_type=MESH)

    @pl.when(z > 0)
    def _():
        pl.semaphore_signal(barrier, inc=1, device_id=at.dzm, device_id_type=MESH)

    pl.semaphore_wait(barrier, len(peers) + (1 - (z + 1) // NZ) + (z + NZ - 1) // NZ)
    loads[0].wait()
    loads[1].wait()

    top = (y + 1) // 4
    low = 1 - (y + 3) // 4
    upper = y // 2
    lp, lm, l2 = 1 - 4 * top, 4 * low - 1, 2 - 4 * upper

    def kv_copy(o, to, send_sem, dev):
        return remote(kvb.at[o + 4, c], kvb.at[to + 4, c], send_sem, kv_r.at[to + 4], dev)

    def kv_sib(o):
        return remote(kvb.at[o + 4, c], kvb.at[o + 4, c], kv_bs.at[o + 4], kv_b.at[o + 4], at.sib)

    kz = [(kv_copy(0, -4, kv_s.at[0], at.dzp), z < NZ - 1), (kv_copy(0, 4, kv_s.at[1], at.dzm), z > 0)]
    ky = [
        kv_copy(0, -lp, kv_s.at[2], at.dyp),
        kv_copy(0, -lm, kv_s.at[3], at.dym),
        kv_copy(0, -l2, kv_s.at[4], at.dy2),
    ]
    for d, ok in kz:
        pl.when(ok)(d.start)
    for d in ky:
        d.start()
    kv_sib(0).start()

    piece = []
    for i in (0, 1):
        rows = pl.ds(pl.multiple_of(16 * (s // 4), 16), 16)
        cols = pl.ds(pl.multiple_of(1024 * i + 256 * lax.rem(s, 4), 256), 256)
        piece.append(remote(wo_hbm.at[rows, cols], wob.at[s, i], o_far.at[0, i], o_far.at[1, i], at.far))
    for d in piece:
        d.start()

    cross_r = remote(res_ref, res_oth, cr.at[0], cr.at[1], at.far)
    gw = Gather(at, wbuf, 48, w_rs, w_rb, w_zs, w_ys, w_bs)
    go = Gather(at, wob, 0, o_rs, o_rb, o_zs, o_ys, o_bs)

    for d in loads[2:5]:
        d.wait()
    gw.zstep(0)

    m_ref[...] = jnp.full(m_ref.shape, -1e30, F32)
    l_ref[...] = jnp.zeros(l_ref.shape, F32)
    acc_ref[...] = jnp.zeros(acc_ref.shape, F32)

    def update(hd, sc, v):
        m_old = m_ref[hd]
        m_new = jnp.maximum(m_old, jnp.max(sc, axis=1, keepdims=True))
        alpha = jnp.exp2(m_old - m_new)
        p = jnp.exp2(sc - m_new[:, 0:1])
        l_ref[hd] = alpha * l_ref[hd] + jnp.sum(p, axis=1, keepdims=True)
        pv = jnp.dot(p.astype(BF16), v, preferred_element_type=F32)
        acc_ref[hd] = alpha * acc_ref[hd] + pv
        m_ref[hd] = m_new

    def bias_of(hd, a, first, kt):
        idx = jnp.clip(first + kt - a + HALF_BAND // TILE, 0, OFFSETS - 1)
        return tab_ref[hd, bk_ref[a, idx]] * LOG2E

    def attend(o, core=None):
        n = 512 if core is None else 256
        first = 4 * o - 2 * c + (0 if core is None else 2 * core)
        for hd in (0, 1):
            head = slice(128 * hd, 128 * hd + 128)
            if core is None:
                k = kvb[o + 4, :, 0, :, head].reshape(n, 128)
                v = kvb[o + 4, :, 1, :, head].reshape(n, 128)
            else:
                k = kvb[o + 4, core, 0, :, head]
                v = kvb[o + 4, core, 1, :, head]
            sc = lax.dot_general(q_ref[:, head], k, (((1,), (1,)), ((), ())), preferred_element_type=F32)
            sc = jnp.concatenate(
                [
                    jnp.concatenate(
                        [
                            sc[128 * a : 128 * a + 128, 128 * kt : 128 * kt + 128] * (SCALE * LOG2E)
                            + bias_of(hd, a, first, kt)
                            for kt in range(n // 128)
                        ],
                        axis=1,
                    )
                    for a in (0, 1)
                ],
                axis=0,
            )
            if core is not None:
                row = lax.broadcasted_iota(jnp.int32, sc.shape, 0)
                col = lax.broadcasted_iota(jnp.int32, sc.shape, 1)
                dist = col - row + first * TILE
                sc = jnp.where(jnp.abs(dist) <= HALF_BAND, sc, -1e30)
            update(hd, sc, v)

    def inside(o):
        return jnp.logical_and(at.chip + o >= 0, at.chip + o < CHIPS)

    def got_own(o):
        kv_copy(o, o, kv_bs.at[0], at.sib).wait_recv()

    def got_sib(o):
        d = remote(kvb.at[o + 4, 1 - c], kvb.at[o + 4, 1 - c], kv_bs.at[o + 4], kv_b.at[o + 4], at.sib)
        d.wait_recv()

    got_sib(0)
    attend(0)

    second = []
    for i, (delta, sgn, dev) in enumerate(
        ((lp, 1 - 2 * top, at.dyp), (lm, 2 * low - 1, at.dym), (l2, 1 - 2 * upper, at.dy2))
    ):
        src = 4 * sgn
        second.append((kv_copy(src, src - delta, kv_s2.at[i], dev), inside(src)))
    for o in (-4, 4):
        pl.when(inside(o))(lambda o=o: got_own(o))
    for d, ok in second:
        pl.when(ok)(d.start)
    for o, keep in ((-4, 1), (4, 0)):
        pl.when(jnp.logical_and(inside(o), c == keep))(lambda o=o: kv_sib(o).start())
    gw.zstep(1)
    gw.ysend(0)
    for i in (0, 1):
        piece[i].wait_recv()
    go.zstep(0)
    go.ysend(0)
    cross_r.start()
    for o, core in ((-4, 0), (-4, 1), (4, 0), (4, 1)):
        need = inside(o)
        if (o, core) == (-4, 0):
            need = jnp.logical_and(need, c == 0)
        if (o, core) == (4, 1):
            need = jnp.logical_and(need, c == 1)

        @pl.when(need)
        def _(o=o, core=core):
            @pl.when(c != core)
            def _():
                got_sib(o)

            attend(o, core)

        if (o, core) == (-4, 1):
            gw.zstep(2)
            gw.ysend(1)
            go.zstep(1)
            go.ysend(1)

    wave1 = [4 * low - 1, 1 - 4 * top, 2 - 4 * upper]
    wave2 = [2 - wave1[0], -2 - wave1[1], -wave1[2]]
    for o in wave1:
        got_own(o)
        kv_sib(o).start()
    gw.zstep(3)
    gw.ysend(2)
    go.zstep(2)
    go.ysend(2)
    for n, o in enumerate(wave1):
        got_sib(o)
        attend(o)
        go.zstep(3 + n)
        go.ysend(3 + n)
        if n == 1:
            gw.zstep(4)
            gw.ysend(3)
    for o in wave2:

        @pl.when(inside(o))
        def _(o=o):
            got_own(o)
            kv_sib(o).start()

    gw.zstep(5)
    gw.ysend(4)
    go.zstep(6)
    go.ysend(6)
    for n, o in enumerate(wave2):

        @pl.when(inside(o))
        def _(o=o):
            got_sib(o)
            attend(o)

    for hd in (0, 1):
        att_own[:, 128 * hd : 128 * hd + 128] = (acc_ref[hd] / l_ref[hd]).astype(BF16)
    half = [pl.ds(0, 128), pl.ds(128, 128)]
    both = (0, 1)
    cross_a = [remote(att_own.at[half[j]], att_oth.at[half[j]], ca.at[0, j], ca.at[1, j], at.far) for j in both]
    for j in both:
        cross_a[j].start()
    gw.zstep(6)
    gw.ysend(5)
    go.zstep(7)
    go.ysend(7)
    loads[5].wait()
    order = (2, 1, 3, 0)

    def colsof(d, i):
        xd = lax.rem(x + d, NX)
        return pl.ds(pl.multiple_of(1024 * i + 256 * xd, 256), 256)

    @pl.loop(0, 4)
    def _(d):
        for i in (0, 1):
            part_ref[d, :, pl.ds(256 * i, 256)] = jnp.dot(
                att_own[...], wo_own[:, colsof(d, i)], preferred_element_type=F32
            )

    @pl.loop(0, NZ)
    def _(k):
        go.yrecv1(k)
        go.yrecv2(k)

    gw.zstep(7)
    gw.ysend(6)
    gw.ysend(7)
    go.wait_other_core()

    @pl.loop(0, 4)
    def _(k):
        gw.yrecv1(k)

    def sums(send, recv, ss, rr, j):
        return [
            remote(send.at[d - 1, half[j]], recv.at[d - 1, half[j]], ss.at[j, d - 1], rr.at[j, d - 1], at.dx[d])
            for d in (1, 2, 3)
        ]

    wob4 = wob.reshape(16, 4, 2, 16, 256)
    rs = [sums(rs_s, rs_r, x1_s, x1_r, j) for j in both]
    for j in both:
        cross_a[j].wait_recv()
        for d in order:
            xd = lax.rem(x + d, NX)
            for i in both:
                w = wob4[:, xd, i].reshape(256, 256)
                cols = pl.ds(256 * i, 256)
                p = part_ref[d, half[j], cols] + jnp.dot(att_oth[half[j], :], w, preferred_element_type=F32)
                if d:
                    rs_s[d - 1, half[j], cols] = p.astype(BF16)
                else:
                    part_ref[0, half[j], cols] = p
            if d:
                rs[j][d - 1].start()

    @pl.loop(4, NZ)
    def _(k):
        gw.yrecv1(k)

    cross_r.wait_recv()
    own = h == 0
    ag = []
    for j in both:
        for d in rs[j]:
            d.wait_recv()
        res0, res1 = res_ref[half[j], :].astype(F32), res_oth[half[j], :].astype(F32)
        for i in both:
            cols = pl.ds(256 * i, 256)
            r = jnp.where(own, res0, res1) if i == 0 else jnp.where(own, res1, res0)
            tot = part_ref[0, half[j], cols] + r
            for d in (1, 2, 3):
                tot += rs_r[d - 1, half[j], cols].astype(F32)
            st_ref[x, half[j], cols] = tot.astype(BF16)

        def slot(xo, d, j=j):
            ref = st_ref.at[xo, half[j]]
            return remote(ref, ref, x2_s.at[j, d - 1], x2_r.at[j, d - 1], at.dx[d])

        for d in (2, 1, 3):
            slot(x, d).start()
            ag.append((slot(x, d), slot(lax.rem(x + 4 - d, NX), d)))

    @pl.loop(0, NZ)
    def _(k):
        gw.yrecv2(k)

    gw.wait_other_core()

    rs2 = [sums(rs2_s, rs2_r, x3_s, x3_r, j) for j in both]
    for j in both:
        for _, d in ag[3 * j : 3 * j + 3]:
            d.wait_recv()
        ssq = jnp.zeros((128, 1), F32)
        for xo in range(NX):
            w = st_ref[xo, half[j], :].astype(F32)
            ssq += jnp.sum(w * w, axis=1, keepdims=True)
        scale = lax.rsqrt(ssq / 2048.0 + 1e-05)
        gate = jnp.zeros((128, FFB), F32)
        up = jnp.zeros((128, FFB), F32)
        for b in range(8):
            hb, xb = b // 4, b % 4
            blk = st_ref[xb, half[j], 256 * hb : 256 * hb + 256].astype(F32)
            nb = (blk * scale * gain_ref[:, 256 * b : 256 * b + 256]).astype(BF16)
            wg = wbuf[8 * b : 8 * b + 8, 0:WROWS, :].reshape(256, FFB)
            wu = wbuf[8 * b : 8 * b + 8, WROWS : 2 * WROWS, :].reshape(256, FFB)
            gate += jnp.dot(nb, wg, preferred_element_type=F32)
            up += jnp.dot(nb, wu, preferred_element_type=F32)
        hidden = (gate / (1.0 + jnp.exp(-gate)) * up).astype(BF16)
        for d in order:
            xd = lax.rem(x + d, NX)
            for i in both:
                w = wbuf[pl.ds(8 * (4 * i + xd), 8), 2 * WROWS : 3 * WROWS, :].reshape(256, FFB)
                p = lax.dot_general(hidden, w, (((1,), (1,)), ((), ())), preferred_element_type=F32)
                cols = pl.ds(256 * i, 256)
                if d:
                    rs2_s[d - 1, half[j], cols] = p.astype(BF16)
                else:
                    part_ref[0, half[j], cols] = p
            if d:
                rs2[j][d - 1].start()

    mine = pl.ds(pl.multiple_of(256 * h, 256), 256)
    theirs = pl.ds(pl.multiple_of(256 * (1 - h), 256), 256)
    cross_f = [remote(fin_s.at[half[j]], fin_r.at[half[j]], cf.at[0, j], cf.at[1, j], at.far) for j in both]

    def total(j, cols):
        tot = part_ref[0, half[j], cols]
        for d in (1, 2, 3):
            tot += rs2_r[d - 1, half[j], cols].astype(F32)
        return tot

    for j in both:
        for d in rs2[j]:
            d.wait_recv()
        fin_s[half[j], :] = total(j, theirs).astype(BF16)
        cross_f[j].start()
    for j in both:
        keep_ref[half[j], :] = total(j, mine) + st_ref[x, half[j], mine].astype(F32)

    for d, ok in kz + second:
        pl.when(ok)(d.wait_send)
    for d in ky + piece + [cross_r] + cross_a + rs[0] + rs[1] + [d for d, _ in ag] + rs2[0] + rs2[1]:
        d.wait_send()
    kv_sib(0).wait_send()
    for o in wave1:
        kv_sib(o).wait_send()
    for o in wave2:
        pl.when(inside(o))(lambda o=o: kv_sib(o).wait_send())
    for o, keep in ((-4, 1), (4, 0)):
        pl.when(jnp.logical_and(inside(o), c == keep))(lambda o=o: kv_sib(o).wait_send())

    @pl.loop(0, NZ)
    def _(k):
        for g in (gw, go):
            g.zstep(k, go=False)
            g.ysend(k, go=False)
            g.yrecv1(k, go=False)
            g.yrecv2(k, go=False)

    for j in both:
        cross_f[j].wait_recv()
        out_ref[half[j], :] = (keep_ref[half[j], :] + fin_r[half[j], :].astype(F32)).astype(BF16)
    for j in both:
        cross_f[j].wait_send()


def shards(queries, keys, values, residual_in, bias_table, buckets, out_weight, gate_weight, up_weight, down_weight_t, norm_gain):
    vmem = pl.BlockSpec(memory_space=pltpu.VMEM)
    smem = pl.BlockSpec(memory_space=pltpu.SMEM)
    hbm = pl.BlockSpec(memory_space=pl.ANY)
    dma = pltpu.SemaphoreType.DMA
    v = pltpu.VMEM
    gather_sems = [dma((CHIPS, 2)), dma((CHIPS,)), dma((CHIPS, 2)), dma((CHIPS, 3)), dma((CHIPS,))]
    scratch = [
        v((9, 2, 2, ROWS, COLS), BF16),
        v((64, 96, FFB), BF16),
        v((64, 2, 16, 256), BF16),
        v((256, 2048), BF16),
        v((ROWS, COLS), BF16),
        v((ROWS, COLS), BF16),
        v((ROWS, COLS), BF16),
        v((2, ROWS, 128), F32),
        v((2, ROWS, 128), F32),
        v((2, ROWS, 128), F32),
        v((4, ROWS, 512), F32),
        v((3, ROWS, 512), BF16),
        v((3, ROWS, 512), BF16),
        v((3, ROWS, 512), BF16),
        v((3, ROWS, 512), BF16),
        v((NX, ROWS, 512), BF16),
        v((ROWS, COLS), BF16),
        v((ROWS, COLS), BF16),
        v((ROWS, COLS), F32),
        dma((6,)), dma((9,)), dma((9,)), dma((5,)), dma((3,)), dma((9,)),
        *gather_sems,
        *gather_sems,
        dma((2, 2)),
        dma((2, 3)), dma((2, 3)), dma((2, 3)), dma((2, 3)), dma((2, 3)), dma((2, 3)),
        dma((2, 2)), dma((2,)), dma((2, 2)),
    ]
    return pl.pallas_call(
        kernel,
        out_shape=jax.ShapeDtypeStruct((ROWS, COLS), BF16),
        in_specs=[vmem, vmem, smem, smem, vmem] + [hbm] * 6,
        out_specs=vmem,
        scratch_shapes=scratch,
        compiler_params=pltpu.CompilerParams(
            collective_id=0, has_side_effects=True, vmem_limit_bytes=60 * 1024 * 1024
        ),
        name="layer",
    )(
        queries, residual_in, bias_table, buckets, norm_gain.reshape(1, -1),
        keys, values, out_weight, gate_weight, up_weight, down_weight_t,
    )


def solution(mesh):
    return jax.shard_map(
        shards,
        mesh=mesh,
        in_specs=(
            P("seq", "tp"),
            P("seq", "tp"),
            P("seq", "tp"),
            P("seq", "tp"),
            P("tp", None),
            P("seq", None),
            P("tp", None),
            P("seq", "tp"),
            P("seq", "tp"),
            P("seq", "tp"),
            P(),
        ),
        out_specs=P("seq", "tp"),
        check_vma=False,
    )
```

```python
import jax
import jax.numpy as jnp
from jax import lax
from jax.experimental import pallas as pl
from jax.experimental.pallas import tpu as pltpu
from jax.sharding import PartitionSpec as P

HEAD_DIM = 128
TILE = 128
HALF_BAND = 2048
OFFSETS = 33
NZ = 8
NY = 4
NX = 4
CHIPS = NZ * NY
ROWS = 256
COLS = 256
FFB = 512
WROWS = 32
SCALE = HEAD_DIM ** (-0.5)
LOG2E = 1.4426950408889634
MESH = pl.DeviceIdType.MESH
F32 = jnp.float32
BF16 = jnp.bfloat16


def remote(src, dst, send_sem, recv_sem, dev):
    return pltpu.make_async_remote_copy(
        src_ref=src,
        dst_ref=dst,
        send_sem=send_sem,
        recv_sem=recv_sem,
        device_id=dev,
        device_id_type=MESH,
    )


class Place:
    def __init__(self):
        s = lax.axis_index("seq")
        t = lax.axis_index("tp")
        self.s, self.t = s, t
        self.c = lax.rem(s, 2)
        self.chip = s // 2
        self.y = lax.rem(self.chip, NY)
        self.z = self.chip // NY
        self.x = lax.rem(t, NX)
        self.h = t // NX
        self.sib = (s + 1 - 2 * self.c, t)
        self.yp = lax.rem(self.y + 1, NY)
        self.ym = lax.rem(self.y + 3, NY)
        self.y2 = lax.rem(self.y + 2, NY)
        self.dyp = self.dev(self.z, self.yp)
        self.dym = self.dev(self.z, self.ym)
        self.dy2 = self.dev(self.z, self.y2)
        self.dzp = self.dev(self.z + 1, self.y)
        self.dzm = self.dev(self.z - 1, self.y)
        self.dx = [None] + [(s, self.h * NX + lax.rem(self.x + d, NX)) for d in (1, 2, 3)]
        self.far = (s, (1 - self.h) * NX + self.x)

    def dev(self, z, y):
        return ((z * NY + y) * 2 + self.c, self.t)


class Gather:
    def __init__(self, at, buf, half, rs, rb, zs, ys, bs):
        self.at, self.buf, self.half = at, buf, half
        self.rs, self.rb, self.zs, self.ys, self.bs = rs, rb, zs, ys, bs

    def full(self, chip, sem, core, send_sem, dev):
        slot = self.buf.at[chip * 2 + core]
        return remote(slot, slot, send_sem, sem, dev)

    def part(self, chip, i, send_sem, dev):
        slot = self.buf.at[chip * 2 + self.at.c, pl.ds(i * self.half, self.half)]
        return remote(slot, slot, send_sem, self.rs.at[chip, i], dev)

    def sib(self, chip):
        return self.full(chip, self.rb.at[chip], self.at.c, self.bs.at[chip], self.at.sib)

    def zstep(self, k, go=True):
        at = self.at
        for way, origin, nxt, dev in (
            (0, at.z - k, at.z + 1, at.dzp),
            (1, at.z + k, at.z - 1, at.dzm),
        ):
            chip = origin * NY + at.y
            valid = jnp.logical_and(origin >= 0, origin < NZ)
            d = self.full(chip, self.rs.at[chip, 0], at.c, self.zs.at[chip, way], dev)

            @pl.when(valid)
            def _(d=d, nxt=nxt):
                if go and not (isinstance(k, int) and k == 0):
                    d.wait_recv()

                @pl.when(jnp.logical_and(nxt >= 0, nxt < NZ))
                def _():
                    if go:
                        d.start()
                    else:
                        d.wait_send()

    def each(self, k, f):
        at = self.at

        @pl.when(at.z - k >= 0)
        def _():
            f(at.z - k)

        @pl.when(jnp.logical_and(k > 0, at.z + k < NZ))
        def _():
            f(at.z + k)

    def ysend(self, k, go=True):
        at = self.at

        def f(zo):
            chip = zo * NY + at.y
            for i, dev in ((0, at.dyp), (1, at.dym)):
                d = self.full(chip, self.rs.at[chip, 0], at.c, self.ys.at[chip, i], dev)
                d.start() if go else d.wait_send()
            d = self.sib(chip)
            d.start() if go else d.wait_send()

        self.each(k, f)

    def yrecv1(self, k, go=True):
        at = self.at

        def f(zo):
            for i, yo, dev in ((0, at.ym, at.dyp), (1, at.yp, at.dym)):
                chip = zo * NY + yo
                d = self.sib(chip)
                if go:
                    self.full(chip, self.rs.at[chip, 0], at.c, self.bs.at[chip], at.sib).wait_recv()
                r = self.part(chip, i, self.ys.at[chip, i], dev)
                r.start() if go else r.wait_send()
                d.start() if go else d.wait_send()

        self.each(k, f)

    def yrecv2(self, k, go=True):
        at = self.at

        def f(zo):
            chip = zo * NY + at.y2
            d = self.sib(chip)
            if go:
                for i in (0, 1):
                    self.part(chip, i, self.bs.at[chip], at.sib).wait_recv()
                d.start()
            else:
                d.wait_send()

        self.each(k, f)

    def wait_other_core(self):
        at = self.at

        @pl.loop(0, CHIPS)
        def _(chip):
            self.full(chip, self.rb.at[chip], 1 - at.c, self.bs.at[chip], at.sib).wait_recv()


class Pieces:
    def __init__(self, at, buf, rs, rb, zs, ys, bs):
        self.at, self.buf = at, buf
        self.rs, self.rb, self.zs, self.ys, self.bs = rs, rb, zs, ys, bs
        self.q = lax.rem(at.z, 4)
        self.base = at.z - self.q

    def copy(self, chip, core, send_sem, recv_sem, dev):
        slot = self.buf.at[chip * 2 + core]
        return remote(slot, slot, send_sem, recv_sem.at[chip], dev)

    def wait(self, chip):
        self.copy(chip, self.at.c, self.bs.at[chip], self.rs, self.at.sib).wait_recv()

    def sib(self, chip):
        return self.copy(chip, self.at.c, self.bs.at[chip], self.rb, self.at.sib)

    def zsend(self, go=True):
        at = self.at
        for d in (1, 3, 2):
            dev = at.dev(self.base + lax.rem(self.q + d, 4), at.y)
            r = self.copy(self.q * NY + at.y, at.c, self.zs.at[d - 1], self.rs, dev)
            r.start() if go else r.wait_send()

    def ysend(self, go=True):
        at = self.at
        for d in range(4):
            chip = lax.rem(self.q + d, 4) * NY + at.y
            if go and d:
                self.wait(chip)
            for i, dev in enumerate((at.dyp, at.dym, at.dy2)):
                r = self.copy(chip, at.c, self.ys.at[d, i], self.rs, dev)
                r.start() if go else r.wait_send()
            r = self.sib(chip)
            r.start() if go else r.wait_send()

    def yrecv(self, go=True):
        at = self.at
        for d in range(4):
            for yo in (at.yp, at.ym, at.y2):
                chip = lax.rem(self.q + d, 4) * NY + yo
                r = self.sib(chip)
                if go:
                    self.wait(chip)
                    r.start()
                else:
                    r.wait_send()

    def wait_other_core(self):
        for chip in range(16):
            self.copy(chip, 1 - self.at.c, self.bs.at[chip], self.rb, self.at.sib).wait_recv()


def kernel(
    q_ref, res_ref, tab_ref, bk_ref, gain_ref, k_hbm, v_hbm, wo_hbm, g_hbm, u_hbm, d_hbm,
    out_ref,
    kvb, wbuf, wob, wo_own, att_own, att_oth, res_oth,
    m_ref, l_ref, acc_ref, part_ref, rs_s, rs_r, rs2_s, rs2_r, st_ref, fin_s, fin_r, keep_ref, hid_ref,
    loc, kv_r, kv_b, kv_s, kv_s2, kv_bs,
    w_rs, w_rb, w_zs, w_ys, w_bs, o_rs, o_rb, o_zs, o_ys, o_bs, o_far,
    x1_s, x1_r, x2_s, x2_r, x3_s, x3_r, ca, cr, cf,
):
    at = Place()
    s, c, x, h, y, z = at.s, at.c, at.x, at.h, at.y, at.z

    loads = [
        pltpu.make_async_copy(k_hbm, kvb.at[4, c, 0], loc.at[0]),
        pltpu.make_async_copy(v_hbm, kvb.at[4, c, 1], loc.at[1]),
        pltpu.make_async_copy(g_hbm, wbuf.at[s, pl.ds(0, WROWS)], loc.at[2]),
        pltpu.make_async_copy(u_hbm, wbuf.at[s, pl.ds(WROWS, WROWS)], loc.at[3]),
        pltpu.make_async_copy(d_hbm, wbuf.at[s, pl.ds(2 * WROWS, WROWS)], loc.at[4]),
        pltpu.make_async_copy(wo_hbm, wo_own, loc.at[5]),
    ]
    for d in loads:
        d.start()

    barrier = pltpu.get_barrier_semaphore()
    quad = [at.dev(z - lax.rem(z, 4) + lax.rem(z + d, 4), y) for d in (1, 2, 3)]
    peers = [at.far] + at.dx[1:] + quad + [at.sib, at.dyp, at.dym, at.dy2]
    for dev in peers:
        pl.semaphore_signal(barrier, inc=1, device_id=dev, device_id_type=MESH)

    @pl.when(z == 3)
    def _():
        pl.semaphore_signal(barrier, inc=1, device_id=at.dzp, device_id_type=MESH)

    @pl.when(z == 4)
    def _():
        pl.semaphore_signal(barrier, inc=1, device_id=at.dzm, device_id_type=MESH)

    m_ref[...] = jnp.full(m_ref.shape, -1e30, F32)
    l_ref[...] = jnp.zeros(l_ref.shape, F32)
    acc_ref[...] = jnp.zeros(acc_ref.shape, F32)
    pl.semaphore_wait(barrier, len(peers) + (z + 1) // 4 - z // 5 - z // 7)
    loads[0].wait()
    loads[1].wait()

    top = (y + 1) // 4
    low = 1 - (y + 3) // 4
    upper = y // 2
    lp, lm, l2 = 1 - 4 * top, 4 * low - 1, 2 - 4 * upper

    def kv_copy(o, to, send_sem, dev):
        return remote(kvb.at[o + 4, c], kvb.at[to + 4, c], send_sem, kv_r.at[to + 4], dev)

    def kv_sib(o):
        return remote(kvb.at[o + 4, c], kvb.at[o + 4, c], kv_bs.at[o + 4], kv_b.at[o + 4], at.sib)

    kz = [(kv_copy(0, -4, kv_s.at[0], at.dzp), z < NZ - 1), (kv_copy(0, 4, kv_s.at[1], at.dzm), z > 0)]
    ky = [
        kv_copy(0, -l2, kv_s.at[4], at.dy2),
        kv_copy(0, -lp, kv_s.at[2], at.dyp),
        kv_copy(0, -lm, kv_s.at[3], at.dym),
    ]
    piece = []
    slot = (lax.rem(z, 4) * NY + y) * 2 + c
    for i in (0, 1):
        rows = pl.ds(pl.multiple_of(32 * (slot // 4), 32), 32)
        cols = pl.ds(pl.multiple_of(1024 * i + 256 * lax.rem(slot, 4), 256), 256)
        piece.append(remote(wo_hbm.at[rows, cols], wob.at[slot, i], o_far.at[0, i], o_far.at[1, i], at.far))
    for d in piece:
        d.start()
    for d, ok in kz:
        pl.when(ok)(d.start)
    for d in ky:
        d.start()
    kv_sib(0).start()

    cross_r = remote(res_ref, res_oth, cr.at[0], cr.at[1], at.far)
    gw = Gather(at, wbuf, 48, w_rs, w_rb, w_zs, w_ys, w_bs)
    go = Pieces(at, wob, o_rs, o_rb, o_zs, o_ys, o_bs)

    for d in loads[2:5]:
        d.wait()
    gw.zstep(0)

    def update(hd, sc, v):
        m_old = m_ref[hd]
        m_new = jnp.maximum(m_old, jnp.max(sc, axis=1, keepdims=True))
        alpha = jnp.exp2(m_old - m_new)
        p = jnp.exp2(sc - m_new[:, 0:1])
        l_ref[hd] = alpha * l_ref[hd] + jnp.sum(p, axis=1, keepdims=True)
        pv = jnp.dot(p.astype(BF16), v, preferred_element_type=F32)
        acc_ref[hd] = alpha * acc_ref[hd] + pv
        m_ref[hd] = m_new

    def bias_of(hd, a, first, kt):
        idx = jnp.clip(first + kt - a + HALF_BAND // TILE, 0, OFFSETS - 1)
        return tab_ref[hd, bk_ref[a, idx]] * LOG2E

    def attend(o, core=None):
        n = 512 if core is None else 256
        first = 4 * o - 2 * c + (0 if core is None else 2 * core)
        for hd in (0, 1):
            head = slice(128 * hd, 128 * hd + 128)
            if core is None:
                k = kvb[o + 4, :, 0, :, head].reshape(n, 128)
                v = kvb[o + 4, :, 1, :, head].reshape(n, 128)
            else:
                k = kvb[o + 4, core, 0, :, head]
                v = kvb[o + 4, core, 1, :, head]
            sc = lax.dot_general(q_ref[:, head], k, (((1,), (1,)), ((), ())), preferred_element_type=F32)
            sc = jnp.concatenate(
                [
                    jnp.concatenate(
                        [
                            sc[128 * a : 128 * a + 128, 128 * kt : 128 * kt + 128] * (SCALE * LOG2E)
                            + bias_of(hd, a, first, kt)
                            for kt in range(n // 128)
                        ],
                        axis=1,
                    )
                    for a in (0, 1)
                ],
                axis=0,
            )
            if core is not None:
                row = lax.broadcasted_iota(jnp.int32, sc.shape, 0)
                col = lax.broadcasted_iota(jnp.int32, sc.shape, 1)
                dist = col - row + first * TILE
                sc = jnp.where(jnp.abs(dist) <= HALF_BAND, sc, -1e30)
            update(hd, sc, v)

    def inside(o):
        return jnp.logical_and(at.chip + o >= 0, at.chip + o < CHIPS)

    def got_own(o):
        kv_copy(o, o, kv_bs.at[0], at.sib).wait_recv()

    def got_sib(o):
        d = remote(kvb.at[o + 4, 1 - c], kvb.at[o + 4, 1 - c], kv_bs.at[o + 4], kv_b.at[o + 4], at.sib)
        d.wait_recv()

    got_sib(0)
    attend(0)

    second = []
    for i, (delta, sgn, dev) in enumerate(((lp, 1 - 2 * top, at.dyp), (lm, 2 * low - 1, at.dym))):
        src = 4 * sgn
        second.append((kv_copy(src, src - delta, kv_s2.at[i], dev), inside(src)))
    near = [2 - 4 * upper, 4 * low - 1, 1 - 4 * top]
    last = [2 - near[1], -2 - near[2], -near[0]]
    zt = z + 1 - 2 * upper
    across = (kv_copy(near[0], -near[0], kv_s2.at[2], at.dev(zt, y)), jnp.logical_and(zt >= 0, zt < NZ))
    for o in (-4, 4):
        pl.when(inside(o))(lambda o=o: got_own(o))
    for d, ok in second:
        pl.when(ok)(d.start)
    for o, keep in ((-4, 1), (4, 0)):
        pl.when(jnp.logical_and(inside(o), c == keep))(lambda o=o: kv_sib(o).start())
    got_own(near[0])
    pl.when(across[1])(across[0].start)
    kv_sib(near[0]).start()
    second.append(across)
    for i in (0, 1):
        piece[i].wait_recv()
    go.zsend()
    gw.zstep(1)
    gw.ysend(0)
    for o, core in ((-4, 0), (-4, 1), (4, 0), (4, 1)):
        need = inside(o)
        if (o, core) == (-4, 0):
            need = jnp.logical_and(need, c == 0)
        if (o, core) == (4, 1):
            need = jnp.logical_and(need, c == 1)

        @pl.when(need)
        def _(o=o, core=core):
            @pl.when(c != core)
            def _():
                got_sib(o)

            attend(o, core)

        if (o, core) == (-4, 1):
            for near_o in near[1:]:
                got_own(near_o)
                kv_sib(near_o).start()
            gw.zstep(2)
            go.ysend()
            cross_r.start()

    gw.ysend(1)
    for n, o in enumerate(near):
        got_sib(o)
        attend(o)
        if n == 0:
            gw.zstep(3)
            gw.ysend(2)
        if n == 2:
            gw.zstep(4)
            gw.ysend(3)
    for o in last:

        @pl.when(inside(o))
        def _(o=o):
            got_own(o)
            kv_sib(o).start()

    gw.zstep(5)
    gw.ysend(4)
    for n, o in enumerate(last):

        @pl.when(inside(o))
        def _(o=o):
            got_sib(o)
            attend(o)

    for hd in (0, 1):
        att_own[:, 128 * hd : 128 * hd + 128] = (acc_ref[hd] / l_ref[hd]).astype(BF16)
    half = [pl.ds(0, 128), pl.ds(128, 128)]
    both = (0, 1)
    cross_a = [remote(att_own.at[half[j]], att_oth.at[half[j]], ca.at[0, j], ca.at[1, j], at.far) for j in both]
    for j in both:
        cross_a[j].start()
    go.yrecv()
    gw.zstep(6)
    gw.ysend(5)
    loads[5].wait()
    order = (2, 1, 3, 0)

    def colsof(d, i):
        xd = lax.rem(x + d, NX)
        return pl.ds(pl.multiple_of(1024 * i + 256 * xd, 256), 256)

    @pl.loop(0, 4)
    def _(d):
        for i in (0, 1):
            part_ref[d, :, pl.ds(256 * i, 256)] = jnp.dot(
                att_own[...], wo_own[:, colsof(d, i)], preferred_element_type=F32
            )

    gw.zstep(7)
    gw.ysend(6)
    gw.ysend(7)
    go.wait_other_core()

    @pl.loop(0, 4)
    def _(k):
        gw.yrecv1(k)

    def sums(send, recv, ss, rr, j):
        return [
            remote(send.at[d - 1, half[j]], recv.at[d - 1, half[j]], ss.at[j, d - 1], rr.at[j, d - 1], at.dx[d])
            for d in (1, 2, 3)
        ]

    wob4 = wob.reshape(8, 4, 2, 32, 256)
    rs = [sums(rs_s, rs_r, x1_s, x1_r, j) for j in both]
    for j in both:
        cross_a[j].wait_recv()
        for d in order:
            xd = lax.rem(x + d, NX)
            for i in both:
                w = wob4[:, xd, i].reshape(256, 256)
                cols = pl.ds(256 * i, 256)
                p = part_ref[d, half[j], cols] + jnp.dot(att_oth[half[j], :], w, preferred_element_type=F32)
                if d:
                    rs_s[d - 1, half[j], cols] = p.astype(BF16)
                else:
                    part_ref[0, half[j], cols] = p
            if d:
                rs[j][d - 1].start()

    @pl.loop(4, NZ)
    def _(k):
        gw.yrecv1(k)

    cross_r.wait_recv()
    own = h == 0
    ag = []
    for j in both:
        for d in rs[j]:
            d.wait_recv()
        res0, res1 = res_ref[half[j], :].astype(F32), res_oth[half[j], :].astype(F32)
        for i in both:
            cols = pl.ds(256 * i, 256)
            r = jnp.where(own, res0, res1) if i == 0 else jnp.where(own, res1, res0)
            tot = part_ref[0, half[j], cols] + r
            for d in (1, 2, 3):
                tot += rs_r[d - 1, half[j], cols].astype(F32)
            st_ref[x, half[j], cols] = tot.astype(BF16)

        def slot(xo, d, j=j):
            ref = st_ref.at[xo, half[j]]
            return remote(ref, ref, x2_s.at[j, d - 1], x2_r.at[j, d - 1], at.dx[d])

        for d in (2, 1, 3):
            slot(x, d).start()
            ag.append((slot(x, d), slot(lax.rem(x + 4 - d, NX), d)))

    @pl.loop(0, NZ)
    def _(k):
        gw.yrecv2(k)

    gw.wait_other_core()

    def sums2(kind, j):
        return [
            remote(
                rs2_s.at[kind, d - 1, half[j]], rs2_r.at[kind, d - 1, half[j]],
                x3_s.at[kind, j, d - 1], x3_r.at[kind, j, d - 1], at.dx[d],
            )
            for d in (1, 2, 3)
        ]

    rs2 = [[sums2(kind, j) for j in both] for kind in both]
    cross_f = [remote(fin_s.at[half[j]], fin_r.at[half[j]], cf.at[0, j], cf.at[1, j], at.far) for j in both]

    def down(kind, j):
        cols = 1 - h if kind == 0 else h
        for d in order:
            xd = lax.rem(x + d, NX)
            w = wbuf[pl.ds(8 * (4 * cols + xd), 8), 2 * WROWS : 3 * WROWS, :].reshape(256, FFB)
            p = lax.dot_general(hid_ref[half[j], :], w, (((1,), (1,)), ((), ())), preferred_element_type=F32)
            if d:
                rs2_s[kind, d - 1, half[j], :] = p.astype(BF16)
                rs2[kind][j][d - 1].start()
            else:
                keep_ref[kind, half[j], :] = p

    def total(kind, j):
        for d in rs2[kind][j]:
            d.wait_recv()
        tot = keep_ref[kind, half[j], :]
        for d in (1, 2, 3):
            tot += rs2_r[kind, d - 1, half[j], :].astype(F32)
        return tot

    def cross(j):
        fin_s[half[j], :] = total(0, j).astype(BF16)
        cross_f[j].start()

    for j in both:
        for _, d in ag[3 * j : 3 * j + 3]:
            d.wait_recv()
        ssq = jnp.zeros((128, 1), F32)
        for xo in range(NX):
            w = st_ref[xo, half[j], :].astype(F32)
            ssq += jnp.sum(w * w, axis=1, keepdims=True)
        scale = lax.rsqrt(ssq / 2048.0 + 1e-05)
        gate = jnp.zeros((128, FFB), F32)
        up = jnp.zeros((128, FFB), F32)
        for b in range(8):
            hb, xb = b // 4, b % 4
            blk = st_ref[xb, half[j], 256 * hb : 256 * hb + 256].astype(F32)
            nb = (blk * scale * gain_ref[:, 256 * b : 256 * b + 256]).astype(BF16)
            wg = wbuf[8 * b : 8 * b + 8, 0:WROWS, :].reshape(256, FFB)
            wu = wbuf[8 * b : 8 * b + 8, WROWS : 2 * WROWS, :].reshape(256, FFB)
            gate += jnp.dot(nb, wg, preferred_element_type=F32)
            up += jnp.dot(nb, wu, preferred_element_type=F32)
        hid_ref[half[j], :] = (gate / (1.0 + jnp.exp(-gate)) * up).astype(BF16)
        if j:
            cross(0)
        down(0, j)

    down(1, 0)
    cross(1)
    down(1, 1)
    mine = pl.ds(pl.multiple_of(256 * h, 256), 256)
    for j in both:
        keep_ref[1, half[j], :] = total(1, j) + st_ref[x, half[j], mine].astype(F32)

    for d, ok in kz + second:
        pl.when(ok)(d.wait_send)
    for d in ky + piece + [cross_r] + cross_a + rs[0] + rs[1] + [d for d, _ in ag] + sum(rs2[0] + rs2[1], []):
        d.wait_send()
    kv_sib(0).wait_send()
    for o in near:
        kv_sib(o).wait_send()
    for o in last:
        pl.when(inside(o))(lambda o=o: kv_sib(o).wait_send())
    for o, keep in ((-4, 1), (4, 0)):
        pl.when(jnp.logical_and(inside(o), c == keep))(lambda o=o: kv_sib(o).wait_send())

    @pl.loop(0, NZ)
    def _(k):
        gw.zstep(k, go=False)
        gw.ysend(k, go=False)
        gw.yrecv1(k, go=False)
        gw.yrecv2(k, go=False)

    go.zsend(go=False)
    go.ysend(go=False)
    go.yrecv(go=False)
    for j in both:
        cross_f[j].wait_recv()
        out_ref[half[j], :] = (keep_ref[1, half[j], :] + fin_r[half[j], :].astype(F32)).astype(BF16)
    for j in both:
        cross_f[j].wait_send()


def shards(queries, keys, values, residual_in, bias_table, buckets, out_weight, gate_weight, up_weight, down_weight_t, norm_gain):
    vmem = pl.BlockSpec(memory_space=pltpu.VMEM)
    smem = pl.BlockSpec(memory_space=pltpu.SMEM)
    hbm = pl.BlockSpec(memory_space=pl.ANY)
    dma = pltpu.SemaphoreType.DMA
    v = pltpu.VMEM
    gather_sems = [dma((CHIPS, 2)), dma((CHIPS,)), dma((CHIPS, 2)), dma((CHIPS, 2)), dma((CHIPS,))]
    scratch = [
        v((9, 2, 2, ROWS, COLS), BF16),
        v((64, 96, FFB), BF16),
        v((32, 2, 32, 256), BF16),
        v((256, 2048), BF16),
        v((ROWS, COLS), BF16),
        v((ROWS, COLS), BF16),
        v((ROWS, COLS), BF16),
        v((2, ROWS, 128), F32),
        v((2, ROWS, 128), F32),
        v((2, ROWS, 128), F32),
        v((4, ROWS, 512), F32),
        v((3, ROWS, 512), BF16),
        v((3, ROWS, 512), BF16),
        v((2, 3, ROWS, COLS), BF16),
        v((2, 3, ROWS, COLS), BF16),
        v((NX, ROWS, 512), BF16),
        v((ROWS, COLS), BF16),
        v((ROWS, COLS), BF16),
        v((2, ROWS, COLS), F32),
        v((ROWS, FFB), BF16),
        dma((6,)), dma((9,)), dma((9,)), dma((5,)), dma((3,)), dma((9,)),
        *gather_sems,
        dma((16,)), dma((16,)), dma((3,)), dma((4, 3)), dma((16,)),
        dma((2, 2)),
        dma((2, 3)), dma((2, 3)), dma((2, 3)), dma((2, 3)), dma((2, 2, 3)), dma((2, 2, 3)),
        dma((2, 2)), dma((2,)), dma((2, 2)),
    ]
    return pl.pallas_call(
        kernel,
        out_shape=jax.ShapeDtypeStruct((ROWS, COLS), BF16),
        in_specs=[vmem, vmem, smem, smem, vmem] + [hbm] * 6,
        out_specs=vmem,
        scratch_shapes=scratch,
        compiler_params=pltpu.CompilerParams(
            collective_id=0, has_side_effects=True, vmem_limit_bytes=60 * 1024 * 1024
        ),
        name="layer",
    )(
        queries, residual_in, bias_table, buckets, norm_gain.reshape(1, -1),
        keys, values, out_weight, gate_weight, up_weight, down_weight_t,
    )


def solution(mesh):
    return jax.shard_map(
        shards,
        mesh=mesh,
        in_specs=(
            P("seq", "tp"),
            P("seq", "tp"),
            P("seq", "tp"),
            P("seq", "tp"),
            P("tp", None),
            P("seq", None),
            P("tp", None),
            P("seq", "tp"),
            P("seq", "tp"),
            P("seq", "tp"),
            P(),
        ),
        out_specs=P("seq", "tp"),
        check_vma=False,
    )
```

```python
import jax
import jax.numpy as jnp
from jax import lax
from jax.experimental import pallas as pl
from jax.experimental.pallas import tpu as pltpu
from jax.sharding import PartitionSpec as P

HEAD_DIM = 128
TILE = 128
HALF_BAND = 2048
OFFSETS = 33
NZ = 8
NY = 4
NX = 4
CHIPS = NZ * NY
ROWS = 256
COLS = 256
FFB = 512
WROWS = 32
SCALE = HEAD_DIM ** (-0.5)
LOG2E = 1.4426950408889634
MESH = pl.DeviceIdType.MESH
F32 = jnp.float32
BF16 = jnp.bfloat16


def remote(src, dst, send_sem, recv_sem, dev):
    return pltpu.make_async_remote_copy(
        src_ref=src,
        dst_ref=dst,
        send_sem=send_sem,
        recv_sem=recv_sem,
        device_id=dev,
        device_id_type=MESH,
    )


class Place:
    def __init__(self):
        s = lax.axis_index("seq")
        t = lax.axis_index("tp")
        self.s, self.t = s, t
        self.c = lax.rem(s, 2)
        self.chip = s // 2
        self.y = lax.rem(self.chip, NY)
        self.z = self.chip // NY
        self.x = lax.rem(t, NX)
        self.h = t // NX
        self.sib = (s + 1 - 2 * self.c, t)
        self.yp = lax.rem(self.y + 1, NY)
        self.ym = lax.rem(self.y + 3, NY)
        self.y2 = lax.rem(self.y + 2, NY)
        self.dyp = self.dev(self.z, self.yp)
        self.dym = self.dev(self.z, self.ym)
        self.dy2 = self.dev(self.z, self.y2)
        self.dzp = self.dev(self.z + 1, self.y)
        self.dzm = self.dev(self.z - 1, self.y)
        self.dx = [None] + [(s, self.h * NX + lax.rem(self.x + d, NX)) for d in (1, 2, 3)]
        self.far = (s, (1 - self.h) * NX + self.x)

    def dev(self, z, y):
        return ((z * NY + y) * 2 + self.c, self.t)


class Gather:
    def __init__(self, at, buf, half, rs, rb, zs, ys, bs):
        self.at, self.buf, self.half = at, buf, half
        self.rs, self.rb, self.zs, self.ys, self.bs = rs, rb, zs, ys, bs

    def full(self, chip, sem, core, send_sem, dev):
        slot = self.buf.at[chip * 2 + core]
        return remote(slot, slot, send_sem, sem, dev)

    def part(self, chip, i, send_sem, dev):
        slot = self.buf.at[chip * 2 + self.at.c, pl.ds(i * self.half, self.half)]
        return remote(slot, slot, send_sem, self.rs.at[chip, i], dev)

    def sib(self, chip):
        return self.full(chip, self.rb.at[chip], self.at.c, self.bs.at[chip], self.at.sib)

    def zstep(self, k, go=True):
        at = self.at
        for way, origin, nxt, dev in (
            (0, at.z - k, at.z + 1, at.dzp),
            (1, at.z + k, at.z - 1, at.dzm),
        ):
            chip = origin * NY + at.y
            valid = jnp.logical_and(origin >= 0, origin < NZ)
            d = self.full(chip, self.rs.at[chip, 0], at.c, self.zs.at[chip, way], dev)

            @pl.when(valid)
            def _(d=d, nxt=nxt):
                if go and not (isinstance(k, int) and k == 0):
                    d.wait_recv()

                @pl.when(jnp.logical_and(nxt >= 0, nxt < NZ))
                def _():
                    if go:
                        d.start()
                    else:
                        d.wait_send()

    def each(self, k, f):
        at = self.at

        @pl.when(at.z - k >= 0)
        def _():
            f(at.z - k)

        @pl.when(jnp.logical_and(k > 0, at.z + k < NZ))
        def _():
            f(at.z + k)

    def ysend(self, k, go=True):
        at = self.at

        def f(zo):
            chip = zo * NY + at.y
            for i, dev in ((0, at.dyp), (1, at.dym)):
                d = self.full(chip, self.rs.at[chip, 0], at.c, self.ys.at[chip, i], dev)
                d.start() if go else d.wait_send()
            d = self.sib(chip)
            d.start() if go else d.wait_send()

        self.each(k, f)

    def yrecv1(self, k, go=True):
        at = self.at

        def f(zo):
            for i, yo, dev in ((0, at.ym, at.dyp), (1, at.yp, at.dym)):
                chip = zo * NY + yo
                d = self.sib(chip)
                if go:
                    self.full(chip, self.rs.at[chip, 0], at.c, self.bs.at[chip], at.sib).wait_recv()
                r = self.part(chip, i, self.ys.at[chip, i], dev)
                r.start() if go else r.wait_send()
                d.start() if go else d.wait_send()

        self.each(k, f)

    def yrecv2(self, k, go=True):
        at = self.at

        def f(zo):
            chip = zo * NY + at.y2
            d = self.sib(chip)
            if go:
                for i in (0, 1):
                    self.part(chip, i, self.bs.at[chip], at.sib).wait_recv()
                d.start()
            else:
                d.wait_send()

        self.each(k, f)

    def wait_other_core(self):
        at = self.at

        @pl.loop(0, CHIPS)
        def _(chip):
            self.full(chip, self.rb.at[chip], 1 - at.c, self.bs.at[chip], at.sib).wait_recv()


def kernel(
    q_ref, res_ref, tab_ref, bk_ref, gain_ref, k_hbm, v_hbm, wo_hbm, g_hbm, u_hbm, d_hbm,
    out_ref,
    kvb, wbuf, wo_own, att_own, mid_s, mid_r,
    m_ref, l_ref, acc_ref, part_ref, rs_s, rs_r, rs2_s, rs2_r, st_ref, fin_s, fin_r, keep_ref, hid_ref,
    loc, kv_r, kv_b, kv_s, kv_s2, kv_bs,
    w_rs, w_rb, w_zs, w_ys, w_bs,
    x1_s, x1_r, x2_s, x2_r, x3_s, x3_r, ca, cf,
):
    at = Place()
    s, c, x, h, y, z = at.s, at.c, at.x, at.h, at.y, at.z

    loads = [
        pltpu.make_async_copy(k_hbm, kvb.at[4, c, 0], loc.at[0]),
        pltpu.make_async_copy(v_hbm, kvb.at[4, c, 1], loc.at[1]),
        pltpu.make_async_copy(g_hbm, wbuf.at[s, pl.ds(0, WROWS)], loc.at[2]),
        pltpu.make_async_copy(u_hbm, wbuf.at[s, pl.ds(WROWS, WROWS)], loc.at[3]),
        pltpu.make_async_copy(d_hbm, wbuf.at[s, pl.ds(2 * WROWS, WROWS)], loc.at[4]),
        pltpu.make_async_copy(wo_hbm, wo_own, loc.at[5]),
    ]
    for d in loads:
        d.start()

    barrier = pltpu.get_barrier_semaphore()
    peers = [at.far] + at.dx[1:] + [at.sib, at.dyp, at.dym, at.dy2]
    for dev in peers:
        pl.semaphore_signal(barrier, inc=1, device_id=dev, device_id_type=MESH)

    @pl.when(z < NZ - 1)
    def _():
        pl.semaphore_signal(barrier, inc=1, device_id=at.dzp, device_id_type=MESH)

    @pl.when(z > 0)
    def _():
        pl.semaphore_signal(barrier, inc=1, device_id=at.dzm, device_id_type=MESH)

    m_ref[...] = jnp.full(m_ref.shape, -1e30, F32)
    l_ref[...] = jnp.zeros(l_ref.shape, F32)
    acc_ref[...] = jnp.zeros(acc_ref.shape, F32)
    pl.semaphore_wait(barrier, len(peers) + (1 - (z + 1) // NZ) + (z + NZ - 1) // NZ)
    loads[0].wait()
    loads[1].wait()

    top = (y + 1) // 4
    low = 1 - (y + 3) // 4
    upper = y // 2
    lp, lm, l2 = 1 - 4 * top, 4 * low - 1, 2 - 4 * upper

    def kv_copy(o, to, send_sem, dev):
        return remote(kvb.at[o + 4, c], kvb.at[to + 4, c], send_sem, kv_r.at[to + 4], dev)

    def kv_sib(o):
        return remote(kvb.at[o + 4, c], kvb.at[o + 4, c], kv_bs.at[o + 4], kv_b.at[o + 4], at.sib)

    kz = [(kv_copy(0, -4, kv_s.at[0], at.dzp), z < NZ - 1), (kv_copy(0, 4, kv_s.at[1], at.dzm), z > 0)]
    ky = [
        kv_copy(0, -l2, kv_s.at[4], at.dy2),
        kv_copy(0, -lp, kv_s.at[2], at.dyp),
        kv_copy(0, -lm, kv_s.at[3], at.dym),
    ]
    for d, ok in kz:
        pl.when(ok)(d.start)
    for d in ky:
        d.start()
    kv_sib(0).start()

    gw = Gather(at, wbuf, 48, w_rs, w_rb, w_zs, w_ys, w_bs)

    for d in loads[2:5]:
        d.wait()
    gw.zstep(0)

    def update(hd, sc, v):
        m_old = m_ref[hd]
        m_new = jnp.maximum(m_old, jnp.max(sc, axis=1, keepdims=True))
        alpha = jnp.exp2(m_old - m_new)
        p = jnp.exp2(sc - m_new[:, 0:1])
        l_ref[hd] = alpha * l_ref[hd] + jnp.sum(p, axis=1, keepdims=True)
        pv = jnp.dot(p.astype(BF16), v, preferred_element_type=F32)
        acc_ref[hd] = alpha * acc_ref[hd] + pv
        m_ref[hd] = m_new

    def bias_of(hd, a, first, kt):
        idx = jnp.clip(first + kt - a + HALF_BAND // TILE, 0, OFFSETS - 1)
        return tab_ref[hd, bk_ref[a, idx]] * LOG2E

    def attend(o, core=None):
        n = 512 if core is None else 256
        first = 4 * o - 2 * c + (0 if core is None else 2 * core)
        for hd in (0, 1):
            head = slice(128 * hd, 128 * hd + 128)
            if core is None:
                k = kvb[o + 4, :, 0, :, head].reshape(n, 128)
                v = kvb[o + 4, :, 1, :, head].reshape(n, 128)
            else:
                k = kvb[o + 4, core, 0, :, head]
                v = kvb[o + 4, core, 1, :, head]
            sc = lax.dot_general(q_ref[:, head], k, (((1,), (1,)), ((), ())), preferred_element_type=F32)
            sc = jnp.concatenate(
                [
                    jnp.concatenate(
                        [
                            sc[128 * a : 128 * a + 128, 128 * kt : 128 * kt + 128] * (SCALE * LOG2E)
                            + bias_of(hd, a, first, kt)
                            for kt in range(n // 128)
                        ],
                        axis=1,
                    )
                    for a in (0, 1)
                ],
                axis=0,
            )
            if core is not None:
                row = lax.broadcasted_iota(jnp.int32, sc.shape, 0)
                col = lax.broadcasted_iota(jnp.int32, sc.shape, 1)
                dist = col - row + first * TILE
                sc = jnp.where(jnp.abs(dist) <= HALF_BAND, sc, -1e30)
            update(hd, sc, v)

    def inside(o):
        return jnp.logical_and(at.chip + o >= 0, at.chip + o < CHIPS)

    def got_own(o):
        kv_copy(o, o, kv_bs.at[0], at.sib).wait_recv()

    def got_sib(o):
        d = remote(kvb.at[o + 4, 1 - c], kvb.at[o + 4, 1 - c], kv_bs.at[o + 4], kv_b.at[o + 4], at.sib)
        d.wait_recv()

    got_sib(0)
    attend(0)

    second = []
    for i, (delta, sgn, dev) in enumerate(((lp, 1 - 2 * top, at.dyp), (lm, 2 * low - 1, at.dym))):
        src = 4 * sgn
        second.append((kv_copy(src, src - delta, kv_s2.at[i], dev), inside(src)))
    near = [2 - 4 * upper, 4 * low - 1, 1 - 4 * top]
    last = [2 - near[1], -2 - near[2], -near[0]]
    zt = z + 1 - 2 * upper
    across = (kv_copy(near[0], -near[0], kv_s2.at[2], at.dev(zt, y)), jnp.logical_and(zt >= 0, zt < NZ))
    for o in (-4, 4):
        pl.when(inside(o))(lambda o=o: got_own(o))
    for d, ok in second:
        pl.when(ok)(d.start)
    for o, keep in ((-4, 1), (4, 0)):
        pl.when(jnp.logical_and(inside(o), c == keep))(lambda o=o: kv_sib(o).start())
    got_own(near[0])
    pl.when(across[1])(across[0].start)
    kv_sib(near[0]).start()
    second.append(across)
    gw.zstep(1)
    gw.ysend(0)
    for o, core in ((-4, 0), (-4, 1), (4, 0), (4, 1)):
        need = inside(o)
        if (o, core) == (-4, 0):
            need = jnp.logical_and(need, c == 0)
        if (o, core) == (4, 1):
            need = jnp.logical_and(need, c == 1)

        @pl.when(need)
        def _(o=o, core=core):
            @pl.when(c != core)
            def _():
                got_sib(o)

            attend(o, core)

        if (o, core) == (-4, 1):
            for near_o in near[1:]:
                got_own(near_o)
                kv_sib(near_o).start()
            gw.zstep(2)

    gw.ysend(1)
    for n, o in enumerate(near):
        got_sib(o)
        attend(o)
        gw.zstep(3 + n)
        gw.ysend(2 + n)
    for o in last:

        @pl.when(inside(o))
        def _(o=o):
            got_own(o)
            kv_sib(o).start()

    gw.zstep(6)
    gw.ysend(5)
    for n, o in enumerate(last):

        @pl.when(inside(o))
        def _(o=o):
            got_sib(o)
            attend(o)

        if n == 0:
            gw.zstep(7)
            gw.ysend(6)
            gw.ysend(7)

    for hd in (0, 1):
        att_own[:, 128 * hd : 128 * hd + 128] = (acc_ref[hd] / l_ref[hd]).astype(BF16)
    half = [pl.ds(0, 128), pl.ds(128, 128)]
    both = (0, 1)
    quart = [pl.ds(64 * j, 64) for j in range(4)]
    loads[5].wait()
    order = (2, 1, 3, 0)

    rs = [
        [
            remote(rs_s.at[d - 1, q], rs_r.at[d - 1, q], x1_s.at[j, d - 1], x1_r.at[j, d - 1], at.dx[d])
            for d in (1, 2, 3)
        ]
        for j, q in enumerate(quart)
    ]
    for j in both:
        for d in order:
            for i in both:
                w = wo_own[:, pl.ds(pl.multiple_of(1024 * i + 256 * lax.rem(x + d, NX), 256), 256)]
                p = jnp.dot(att_own[half[j], :], w, preferred_element_type=F32)
                cols = pl.ds(256 * i, 256)
                if d:
                    rs_s[d - 1, half[j], cols] = p.astype(BF16)
                else:
                    part_ref[half[j], cols] = p
            if d:
                rs[2 * j][d - 1].start()
        for d in (2, 1, 3):
            rs[2 * j + 1][d - 1].start()

    cross_a = [remote(mid_s.at[q], mid_r.at[q], ca.at[0, j], ca.at[1, j], at.far) for j, q in enumerate(quart)]
    for j, q in enumerate(quart):
        for d in rs[j]:
            d.wait_recv()
        res = res_ref[q, :].astype(F32)
        for i in both:
            cols = pl.ds(256 * i, 256)
            tot = part_ref[q, cols] + jnp.where(h == i, res, 0.0)
            for d in (1, 2, 3):
                tot += rs_r[d - 1, q, cols].astype(F32)
            mid_s[q, cols] = tot.astype(BF16)
        cross_a[j].start()

    @pl.loop(0, NZ)
    def _(k):
        gw.yrecv1(k)

    @pl.loop(0, NZ)
    def _(k):
        gw.yrecv2(k)

    ag = []
    for j, q in enumerate(quart):
        cross_a[j].wait_recv()
        st_ref[x, q, :] = (mid_s[q, :].astype(F32) + mid_r[q, :].astype(F32)).astype(BF16)

        def share(xo, d, j=j, q=q):
            ref = st_ref.at[xo, q]
            return remote(ref, ref, x2_s.at[j, d - 1], x2_r.at[j, d - 1], at.dx[d])

        for d in (2, 1, 3):
            share(x, d).start()
            ag.append((share(x, d), share(lax.rem(x + 4 - d, NX), d)))

    gw.wait_other_core()

    def sums2(kind, j):
        return [
            remote(
                rs2_s.at[kind, d - 1, half[j]], rs2_r.at[kind, d - 1, half[j]],
                x3_s.at[kind, j, d - 1], x3_r.at[kind, j, d - 1], at.dx[d],
            )
            for d in (1, 2, 3)
        ]

    rs2 = [[sums2(kind, j) for j in both] for kind in both]
    cross_f = [remote(fin_s.at[half[j]], fin_r.at[half[j]], cf.at[0, j], cf.at[1, j], at.far) for j in both]

    def down(kind, j):
        cols = 1 - h if kind == 0 else h
        for d in order:
            xd = lax.rem(x + d, NX)
            w = wbuf[pl.ds(8 * (4 * cols + xd), 8), 2 * WROWS : 3 * WROWS, :].reshape(256, FFB)
            p = lax.dot_general(hid_ref[half[j], :], w, (((1,), (1,)), ((), ())), preferred_element_type=F32)
            if d:
                rs2_s[kind, d - 1, half[j], :] = p.astype(BF16)
                rs2[kind][j][d - 1].start()
            else:
                keep_ref[kind, half[j], :] = p

    def total(kind, j):
        for d in rs2[kind][j]:
            d.wait_recv()
        tot = keep_ref[kind, half[j], :]
        for d in (1, 2, 3):
            tot += rs2_r[kind, d - 1, half[j], :].astype(F32)
        return tot

    def cross(j):
        fin_s[half[j], :] = total(0, j).astype(BF16)
        cross_f[j].start()

    for j in both:
        for _, d in ag[6 * j : 6 * j + 6]:
            d.wait_recv()
        ssq = jnp.zeros((128, 1), F32)
        for xo in range(NX):
            w = st_ref[xo, half[j], :].astype(F32)
            ssq += jnp.sum(w * w, axis=1, keepdims=True)
        scale = lax.rsqrt(ssq / 2048.0 + 1e-05)
        gate = jnp.zeros((128, FFB), F32)
        up = jnp.zeros((128, FFB), F32)
        for b in range(8):
            hb, xb = b // 4, b % 4
            blk = st_ref[xb, half[j], 256 * hb : 256 * hb + 256].astype(F32)
            nb = (blk * scale * gain_ref[:, 256 * b : 256 * b + 256]).astype(BF16)
            wg = wbuf[8 * b : 8 * b + 8, 0:WROWS, :].reshape(256, FFB)
            wu = wbuf[8 * b : 8 * b + 8, WROWS : 2 * WROWS, :].reshape(256, FFB)
            gate += jnp.dot(nb, wg, preferred_element_type=F32)
            up += jnp.dot(nb, wu, preferred_element_type=F32)
        hid_ref[half[j], :] = (gate / (1.0 + jnp.exp(-gate)) * up).astype(BF16)
        if j:
            cross(0)
        down(0, j)

    down(1, 0)
    cross(1)
    down(1, 1)
    mine = pl.ds(pl.multiple_of(256 * h, 256), 256)
    for j in both:
        keep_ref[1, half[j], :] = total(1, j) + st_ref[x, half[j], mine].astype(F32)

    for d, ok in kz + second:
        pl.when(ok)(d.wait_send)
    for d in ky + cross_a + sum(rs, []) + [d for d, _ in ag] + sum(rs2[0] + rs2[1], []):
        d.wait_send()
    kv_sib(0).wait_send()
    for o in near:
        kv_sib(o).wait_send()
    for o in last:
        pl.when(inside(o))(lambda o=o: kv_sib(o).wait_send())
    for o, keep in ((-4, 1), (4, 0)):
        pl.when(jnp.logical_and(inside(o), c == keep))(lambda o=o: kv_sib(o).wait_send())

    @pl.loop(0, NZ)
    def _(k):
        gw.zstep(k, go=False)
        gw.ysend(k, go=False)
        gw.yrecv1(k, go=False)
        gw.yrecv2(k, go=False)

    for j in both:
        cross_f[j].wait_recv()
        out_ref[half[j], :] = (keep_ref[1, half[j], :] + fin_r[half[j], :].astype(F32)).astype(BF16)
    for j in both:
        cross_f[j].wait_send()


def shards(queries, keys, values, residual_in, bias_table, buckets, out_weight, gate_weight, up_weight, down_weight_t, norm_gain):
    vmem = pl.BlockSpec(memory_space=pltpu.VMEM)
    smem = pl.BlockSpec(memory_space=pltpu.SMEM)
    hbm = pl.BlockSpec(memory_space=pl.ANY)
    dma = pltpu.SemaphoreType.DMA
    v = pltpu.VMEM
    gather_sems = [dma((CHIPS, 2)), dma((CHIPS,)), dma((CHIPS, 2)), dma((CHIPS, 2)), dma((CHIPS,))]
    scratch = [
        v((9, 2, 2, ROWS, COLS), BF16),
        v((64, 96, FFB), BF16),
        v((256, 2048), BF16),
        v((ROWS, COLS), BF16),
        v((ROWS, 512), BF16),
        v((ROWS, 512), BF16),
        v((2, ROWS, 128), F32),
        v((2, ROWS, 128), F32),
        v((2, ROWS, 128), F32),
        v((ROWS, 512), F32),
        v((3, ROWS, 512), BF16),
        v((3, ROWS, 512), BF16),
        v((2, 3, ROWS, COLS), BF16),
        v((2, 3, ROWS, COLS), BF16),
        v((NX, ROWS, 512), BF16),
        v((ROWS, COLS), BF16),
        v((ROWS, COLS), BF16),
        v((2, ROWS, COLS), F32),
        v((ROWS, FFB), BF16),
        dma((6,)), dma((9,)), dma((9,)), dma((5,)), dma((3,)), dma((9,)),
        *gather_sems,
        dma((4, 3)), dma((4, 3)), dma((4, 3)), dma((4, 3)), dma((2, 2, 3)), dma((2, 2, 3)),
        dma((2, 4)), dma((2, 2)),
    ]
    return pl.pallas_call(
        kernel,
        out_shape=jax.ShapeDtypeStruct((ROWS, COLS), BF16),
        in_specs=[vmem, vmem, smem, smem, vmem] + [hbm] * 6,
        out_specs=vmem,
        scratch_shapes=scratch,
        compiler_params=pltpu.CompilerParams(
            collective_id=0, has_side_effects=True, vmem_limit_bytes=60 * 1024 * 1024
        ),
        name="layer",
    )(
        queries, residual_in, bias_table, buckets, norm_gain.reshape(1, -1),
        keys, values, out_weight, gate_weight, up_weight, down_weight_t,
    )


def solution(mesh):
    return jax.shard_map(
        shards,
        mesh=mesh,
        in_specs=(
            P("seq", "tp"),
            P("seq", "tp"),
            P("seq", "tp"),
            P("seq", "tp"),
            P("tp", None),
            P("seq", None),
            P("tp", None),
            P("seq", "tp"),
            P("seq", "tp"),
            P("seq", "tp"),
            P(),
        ),
        out_specs=P("seq", "tp"),
        check_vma=False,
    )
```

```python
import jax
import jax.numpy as jnp
from jax import lax
from jax.experimental import pallas as pl
from jax.experimental.pallas import tpu as pltpu
from jax.sharding import PartitionSpec as P

HEAD_DIM = 128
TILE = 128
HALF_BAND = 2048
OFFSETS = 33
NZ = 8
NY = 4
NX = 4
CHIPS = NZ * NY
ROWS = 256
COLS = 256
FFB = 512
WROWS = 32
SCALE = HEAD_DIM ** (-0.5)
LOG2E = 1.4426950408889634
MESH = pl.DeviceIdType.MESH
F32 = jnp.float32
BF16 = jnp.bfloat16


def remote(src, dst, send_sem, recv_sem, dev):
    return pltpu.make_async_remote_copy(
        src_ref=src,
        dst_ref=dst,
        send_sem=send_sem,
        recv_sem=recv_sem,
        device_id=dev,
        device_id_type=MESH,
    )


class Place:
    def __init__(self):
        s = lax.axis_index("seq")
        t = lax.axis_index("tp")
        self.s, self.t = s, t
        self.c = lax.rem(s, 2)
        self.chip = s // 2
        self.y = lax.rem(self.chip, NY)
        self.z = self.chip // NY
        self.x = lax.rem(t, NX)
        self.h = t // NX
        self.sib = (s + 1 - 2 * self.c, t)
        self.yp = lax.rem(self.y + 1, NY)
        self.ym = lax.rem(self.y + 3, NY)
        self.y2 = lax.rem(self.y + 2, NY)
        self.dyp = self.dev(self.z, self.yp)
        self.dym = self.dev(self.z, self.ym)
        self.dy2 = self.dev(self.z, self.y2)
        self.dzp = self.dev(self.z + 1, self.y)
        self.dzm = self.dev(self.z - 1, self.y)
        self.dx = [None] + [(s, self.h * NX + lax.rem(self.x + d, NX)) for d in (1, 2, 3)]
        self.far = (s, (1 - self.h) * NX + self.x)

    def dev(self, z, y):
        return ((z * NY + y) * 2 + self.c, self.t)


class Gather:
    def __init__(self, at, buf, half, rs, rb, zs, ys, bs):
        self.at, self.buf, self.half = at, buf, half
        self.rs, self.rb, self.zs, self.ys, self.bs = rs, rb, zs, ys, bs

    def full(self, chip, sem, core, send_sem, dev):
        slot = self.buf.at[chip * 2 + core]
        return remote(slot, slot, send_sem, sem, dev)

    def part(self, chip, i, send_sem, dev):
        slot = self.buf.at[chip * 2 + self.at.c, pl.ds(i * self.half, self.half)]
        return remote(slot, slot, send_sem, self.rs.at[chip, i], dev)

    def sib(self, chip):
        return self.full(chip, self.rb.at[chip], self.at.c, self.bs.at[chip], self.at.sib)

    def zstep(self, k, go=True):
        at = self.at
        for way, origin, nxt, dev in (
            (0, at.z - k, at.z + 1, at.dzp),
            (1, at.z + k, at.z - 1, at.dzm),
        ):
            chip = origin * NY + at.y
            valid = jnp.logical_and(origin >= 0, origin < NZ)
            d = self.full(chip, self.rs.at[chip, 0], at.c, self.zs.at[chip, way], dev)

            @pl.when(valid)
            def _(d=d, nxt=nxt):
                if go and not (isinstance(k, int) and k == 0):
                    d.wait_recv()

                @pl.when(jnp.logical_and(nxt >= 0, nxt < NZ))
                def _():
                    if go:
                        d.start()
                    else:
                        d.wait_send()

    def each(self, k, f):
        at = self.at

        @pl.when(at.z - k >= 0)
        def _():
            f(at.z - k)

        @pl.when(jnp.logical_and(k > 0, at.z + k < NZ))
        def _():
            f(at.z + k)

    def ysend(self, k, go=True):
        at = self.at

        def f(zo):
            chip = zo * NY + at.y
            for i, dev in ((0, at.dyp), (1, at.dym)):
                d = self.full(chip, self.rs.at[chip, 0], at.c, self.ys.at[chip, i], dev)
                d.start() if go else d.wait_send()
            d = self.sib(chip)
            d.start() if go else d.wait_send()

        self.each(k, f)

    def yrecv1(self, k, go=True):
        at = self.at

        def f(zo):
            for i, yo, dev in ((0, at.ym, at.dyp), (1, at.yp, at.dym)):
                chip = zo * NY + yo
                d = self.sib(chip)
                if go:
                    self.full(chip, self.rs.at[chip, 0], at.c, self.bs.at[chip], at.sib).wait_recv()
                r = self.part(chip, i, self.ys.at[chip, i], dev)
                r.start() if go else r.wait_send()
                d.start() if go else d.wait_send()

        self.each(k, f)

    def yrecv2(self, k, go=True):
        at = self.at

        def f(zo):
            chip = zo * NY + at.y2
            d = self.sib(chip)
            if go:
                for i in (0, 1):
                    self.part(chip, i, self.bs.at[chip], at.sib).wait_recv()
                d.start()
            else:
                d.wait_send()

        self.each(k, f)

    def wait_other_core(self):
        at = self.at

        @pl.loop(0, CHIPS)
        def _(chip):
            self.full(chip, self.rb.at[chip], 1 - at.c, self.bs.at[chip], at.sib).wait_recv()


def kernel(
    q_ref, res_ref, tab_ref, bk_ref, gain_ref, k_hbm, v_hbm, wo_hbm, g_hbm, u_hbm, d_hbm,
    out_ref,
    kvb, wbuf, wo_own, att_own, mid_s, mid_r,
    m_ref, l_ref, acc_ref, part_ref, rs_s, rs_r, rs2_s, rs2_r, st_ref, fin_s, fin_r, keep_ref, hid_ref,
    loc, kv_r, kv_b, kv_s, kv_s2, kv_bs,
    w_rs, w_rb, w_zs, w_ys, w_bs,
    x1_s, x1_r, x2_s, x2_r, x3_s, x3_r, ca, cf,
):
    at = Place()
    s, c, x, h, y, z = at.s, at.c, at.x, at.h, at.y, at.z

    loads = [
        pltpu.make_async_copy(k_hbm, kvb.at[4, c, 0], loc.at[0]),
        pltpu.make_async_copy(v_hbm, kvb.at[4, c, 1], loc.at[1]),
        pltpu.make_async_copy(g_hbm, wbuf.at[s, pl.ds(0, WROWS)], loc.at[2]),
        pltpu.make_async_copy(u_hbm, wbuf.at[s, pl.ds(WROWS, WROWS)], loc.at[3]),
        pltpu.make_async_copy(d_hbm, wbuf.at[s, pl.ds(2 * WROWS, WROWS)], loc.at[4]),
        pltpu.make_async_copy(wo_hbm, wo_own, loc.at[5]),
    ]
    for d in loads:
        d.start()

    barrier = pltpu.get_barrier_semaphore()
    peers = [at.far] + at.dx[1:] + [at.sib, at.dyp, at.dym, at.dy2]
    for dev in peers:
        pl.semaphore_signal(barrier, inc=1, device_id=dev, device_id_type=MESH)

    @pl.when(z < NZ - 1)
    def _():
        pl.semaphore_signal(barrier, inc=1, device_id=at.dzp, device_id_type=MESH)

    @pl.when(z > 0)
    def _():
        pl.semaphore_signal(barrier, inc=1, device_id=at.dzm, device_id_type=MESH)

    m_ref[...] = jnp.full(m_ref.shape, -1e30, F32)
    l_ref[...] = jnp.zeros(l_ref.shape, F32)
    acc_ref[...] = jnp.zeros(acc_ref.shape, F32)
    pl.semaphore_wait(barrier, len(peers) + (1 - (z + 1) // NZ) + (z + NZ - 1) // NZ)
    loads[0].wait()
    loads[1].wait()

    top = (y + 1) // 4
    low = 1 - (y + 3) // 4
    upper = y // 2
    lp, lm, l2 = 1 - 4 * top, 4 * low - 1, 2 - 4 * upper

    def kv_copy(o, to, send_sem, dev):
        return remote(kvb.at[o + 4, c], kvb.at[to + 4, c], send_sem, kv_r.at[to + 4], dev)

    def kv_sib(o):
        return remote(kvb.at[o + 4, c], kvb.at[o + 4, c], kv_bs.at[o + 4], kv_b.at[o + 4], at.sib)

    kz = [(kv_copy(0, -4, kv_s.at[0], at.dzp), z < NZ - 1), (kv_copy(0, 4, kv_s.at[1], at.dzm), z > 0)]
    ky = [
        kv_copy(0, -l2, kv_s.at[4], at.dy2),
        kv_copy(0, -lp, kv_s.at[2], at.dyp),
        kv_copy(0, -lm, kv_s.at[3], at.dym),
    ]
    for d, ok in kz:
        pl.when(ok)(d.start)
    for d in ky:
        d.start()
    kv_sib(0).start()

    gw = Gather(at, wbuf, 48, w_rs, w_rb, w_zs, w_ys, w_bs)

    for d in loads[2:5]:
        d.wait()
    gw.zstep(0)

    def update(hd, sc, v):
        m_old = m_ref[hd]
        m_new = jnp.maximum(m_old, jnp.max(sc, axis=1, keepdims=True))
        alpha = jnp.exp2(m_old - m_new)
        p = jnp.exp2(sc - m_new[:, 0:1])
        l_ref[hd] = alpha * l_ref[hd] + jnp.sum(p, axis=1, keepdims=True)
        pv = jnp.dot(p.astype(BF16), v, preferred_element_type=F32)
        acc_ref[hd] = alpha * acc_ref[hd] + pv
        m_ref[hd] = m_new

    def bias_of(hd, a, first, kt):
        idx = jnp.clip(first + kt - a + HALF_BAND // TILE, 0, OFFSETS - 1)
        return tab_ref[hd, bk_ref[a, idx]] * LOG2E

    def attend(o, core=None):
        n = 512 if core is None else 256
        first = 4 * o - 2 * c + (0 if core is None else 2 * core)
        for hd in (0, 1):
            head = slice(128 * hd, 128 * hd + 128)
            if core is None:
                k = kvb[o + 4, :, 0, :, head].reshape(n, 128)
                v = kvb[o + 4, :, 1, :, head].reshape(n, 128)
            else:
                k = kvb[o + 4, core, 0, :, head]
                v = kvb[o + 4, core, 1, :, head]
            sc = lax.dot_general(q_ref[:, head], k, (((1,), (1,)), ((), ())), preferred_element_type=F32)
            sc = jnp.concatenate(
                [
                    jnp.concatenate(
                        [
                            sc[128 * a : 128 * a + 128, 128 * kt : 128 * kt + 128] * (SCALE * LOG2E)
                            + bias_of(hd, a, first, kt)
                            for kt in range(n // 128)
                        ],
                        axis=1,
                    )
                    for a in (0, 1)
                ],
                axis=0,
            )
            if core is not None:
                row = lax.broadcasted_iota(jnp.int32, sc.shape, 0)
                col = lax.broadcasted_iota(jnp.int32, sc.shape, 1)
                dist = col - row + first * TILE
                sc = jnp.where(jnp.abs(dist) <= HALF_BAND, sc, -1e30)
            update(hd, sc, v)

    def inside(o):
        return jnp.logical_and(at.chip + o >= 0, at.chip + o < CHIPS)

    def got_own(o):
        kv_copy(o, o, kv_bs.at[0], at.sib).wait_recv()

    def got_sib(o):
        d = remote(kvb.at[o + 4, 1 - c], kvb.at[o + 4, 1 - c], kv_bs.at[o + 4], kv_b.at[o + 4], at.sib)
        d.wait_recv()

    got_sib(0)
    attend(0)

    second = []
    for i, (delta, sgn, dev) in enumerate(((lp, 1 - 2 * top, at.dyp), (lm, 2 * low - 1, at.dym))):
        src = 4 * sgn
        second.append((kv_copy(src, src - delta, kv_s2.at[i], dev), inside(src)))
    near = [2 - 4 * upper, 4 * low - 1, 1 - 4 * top]
    last = [2 - near[1], -2 - near[2], -near[0]]
    zt = z + 1 - 2 * upper
    across = (kv_copy(near[0], -near[0], kv_s2.at[2], at.dev(zt, y)), jnp.logical_and(zt >= 0, zt < NZ))
    for o in (-4, 4):
        pl.when(inside(o))(lambda o=o: got_own(o))
    for d, ok in second:
        pl.when(ok)(d.start)
    for o, keep in ((-4, 1), (4, 0)):
        pl.when(jnp.logical_and(inside(o), c == keep))(lambda o=o: kv_sib(o).start())
    got_own(near[0])
    pl.when(across[1])(across[0].start)
    kv_sib(near[0]).start()
    second.append(across)
    for o, core in ((-4, 0), (-4, 1), (4, 0), (4, 1)):
        need = inside(o)
        if (o, core) == (-4, 0):
            need = jnp.logical_and(need, c == 0)
        if (o, core) == (4, 1):
            need = jnp.logical_and(need, c == 1)

        @pl.when(need)
        def _(o=o, core=core):
            @pl.when(c != core)
            def _():
                got_sib(o)

            attend(o, core)

        if (o, core) == (-4, 1):
            for near_o in near[1:]:
                got_own(near_o)
                kv_sib(near_o).start()
            gw.zstep(1)
            gw.ysend(0)

    for n, o in enumerate(near):
        got_sib(o)
        attend(o)
        if n == 0:
            gw.zstep(2)
            gw.ysend(1)
        if n == 1:
            gw.zstep(3)
            gw.ysend(2)
        if n == 2:
            gw.zstep(4)
            gw.ysend(3)
    for o in last:

        @pl.when(inside(o))
        def _(o=o):
            got_own(o)
            kv_sib(o).start()

    gw.zstep(5)
    gw.ysend(4)
    for n, o in enumerate(last):

        @pl.when(inside(o))
        def _(o=o):
            got_sib(o)
            attend(o)

        if n == 0:
            gw.zstep(6)
            gw.ysend(5)

    for hd in (0, 1):
        att_own[:, 128 * hd : 128 * hd + 128] = (acc_ref[hd] / l_ref[hd]).astype(BF16)
    half = [pl.ds(0, 128), pl.ds(128, 128)]
    both = (0, 1)
    quart = [pl.ds(64 * j, 64) for j in range(4)]
    loads[5].wait()
    order = (2, 1, 3, 0)

    rs = [
        [
            remote(rs_s.at[d - 1, q], rs_r.at[d - 1, q], x1_s.at[j, d - 1], x1_r.at[j, d - 1], at.dx[d])
            for d in (1, 2, 3)
        ]
        for j, q in enumerate(quart)
    ]
    for j in both:
        for d in order:
            for i in both:
                w = wo_own[:, pl.ds(pl.multiple_of(1024 * i + 256 * lax.rem(x + d, NX), 256), 256)]
                p = jnp.dot(att_own[half[j], :], w, preferred_element_type=F32)
                cols = pl.ds(256 * i, 256)
                if d:
                    rs_s[d - 1, half[j], cols] = p.astype(BF16)
                else:
                    part_ref[half[j], cols] = p
            if d:
                rs[2 * j][d - 1].start()
        for d in (2, 1, 3):
            rs[2 * j + 1][d - 1].start()

    gw.zstep(7)
    gw.ysend(6)
    gw.ysend(7)
    cross_a = [remote(mid_s.at[q], mid_r.at[q], ca.at[0, j], ca.at[1, j], at.far) for j, q in enumerate(quart)]
    for j, q in enumerate(quart):
        for d in rs[j]:
            d.wait_recv()
        res = res_ref[q, :].astype(F32)
        for i in both:
            cols = pl.ds(256 * i, 256)
            tot = part_ref[q, cols] + jnp.where(h == i, res, 0.0)
            for d in (1, 2, 3):
                tot += rs_r[d - 1, q, cols].astype(F32)
            mid_s[q, cols] = tot.astype(BF16)
        cross_a[j].start()

    @pl.loop(0, NZ)
    def _(k):
        gw.yrecv1(k)

    @pl.loop(0, NZ)
    def _(k):
        gw.yrecv2(k)

    ag = []
    for j, q in enumerate(quart):
        cross_a[j].wait_recv()
        st_ref[x, q, :] = (mid_s[q, :].astype(F32) + mid_r[q, :].astype(F32)).astype(BF16)

        def share(xo, d, j=j, q=q):
            ref = st_ref.at[xo, q]
            return remote(ref, ref, x2_s.at[j, d - 1], x2_r.at[j, d - 1], at.dx[d])

        for d in (2, 1, 3):
            share(x, d).start()
            ag.append((share(x, d), share(lax.rem(x + 4 - d, NX), d)))

    gw.wait_other_core()

    def sums2(kind, j):
        return [
            remote(
                rs2_s.at[kind, d - 1, half[j]], rs2_r.at[kind, d - 1, half[j]],
                x3_s.at[kind, j, d - 1], x3_r.at[kind, j, d - 1], at.dx[d],
            )
            for d in (1, 2, 3)
        ]

    rs2 = [[sums2(kind, j) for j in both] for kind in both]
    cross_f = [remote(fin_s.at[half[j]], fin_r.at[half[j]], cf.at[0, j], cf.at[1, j], at.far) for j in both]

    def down(kind, j):
        cols = 1 - h if kind == 0 else h
        for d in order:
            xd = lax.rem(x + d, NX)
            w = wbuf[pl.ds(8 * (4 * cols + xd), 8), 2 * WROWS : 3 * WROWS, :].reshape(256, FFB)
            p = lax.dot_general(hid_ref[half[j], :], w, (((1,), (1,)), ((), ())), preferred_element_type=F32)
            if d:
                rs2_s[kind, d - 1, half[j], :] = p.astype(BF16)
                rs2[kind][j][d - 1].start()
            else:
                keep_ref[kind, half[j], :] = p

    def total(kind, j):
        for d in rs2[kind][j]:
            d.wait_recv()
        tot = keep_ref[kind, half[j], :]
        for d in (1, 2, 3):
            tot += rs2_r[kind, d - 1, half[j], :].astype(F32)
        return tot

    def cross(j):
        fin_s[half[j], :] = total(0, j).astype(BF16)
        cross_f[j].start()

    for j in both:
        for _, d in ag[6 * j : 6 * j + 6]:
            d.wait_recv()
        ssq = jnp.zeros((128, 1), F32)
        for xo in range(NX):
            w = st_ref[xo, half[j], :].astype(F32)
            ssq += jnp.sum(w * w, axis=1, keepdims=True)
        scale = lax.rsqrt(ssq / 2048.0 + 1e-05)
        gate = jnp.zeros((128, FFB), F32)
        up = jnp.zeros((128, FFB), F32)
        for b in range(8):
            hb, xb = b // 4, b % 4
            blk = st_ref[xb, half[j], 256 * hb : 256 * hb + 256].astype(F32)
            nb = (blk * scale * gain_ref[:, 256 * b : 256 * b + 256]).astype(BF16)
            wg = wbuf[8 * b : 8 * b + 8, 0:WROWS, :].reshape(256, FFB)
            wu = wbuf[8 * b : 8 * b + 8, WROWS : 2 * WROWS, :].reshape(256, FFB)
            gate += jnp.dot(nb, wg, preferred_element_type=F32)
            up += jnp.dot(nb, wu, preferred_element_type=F32)
        hid_ref[half[j], :] = (gate / (1.0 + jnp.exp(-gate)) * up).astype(BF16)
        if j:
            cross(0)
        down(0, j)

    down(1, 0)
    cross(1)
    down(1, 1)
    mine = pl.ds(pl.multiple_of(256 * h, 256), 256)
    for j in both:
        keep_ref[1, half[j], :] = total(1, j) + st_ref[x, half[j], mine].astype(F32)

    for d, ok in kz + second:
        pl.when(ok)(d.wait_send)
    for d in ky + cross_a + sum(rs, []) + [d for d, _ in ag] + sum(rs2[0] + rs2[1], []):
        d.wait_send()
    kv_sib(0).wait_send()
    for o in near:
        kv_sib(o).wait_send()
    for o in last:
        pl.when(inside(o))(lambda o=o: kv_sib(o).wait_send())
    for o, keep in ((-4, 1), (4, 0)):
        pl.when(jnp.logical_and(inside(o), c == keep))(lambda o=o: kv_sib(o).wait_send())

    @pl.loop(0, NZ)
    def _(k):
        gw.zstep(k, go=False)
        gw.ysend(k, go=False)
        gw.yrecv1(k, go=False)
        gw.yrecv2(k, go=False)

    for j in both:
        cross_f[j].wait_recv()
        out_ref[half[j], :] = (keep_ref[1, half[j], :] + fin_r[half[j], :].astype(F32)).astype(BF16)
    for j in both:
        cross_f[j].wait_send()


def shards(queries, keys, values, residual_in, bias_table, buckets, out_weight, gate_weight, up_weight, down_weight_t, norm_gain):
    vmem = pl.BlockSpec(memory_space=pltpu.VMEM)
    smem = pl.BlockSpec(memory_space=pltpu.SMEM)
    hbm = pl.BlockSpec(memory_space=pl.ANY)
    dma = pltpu.SemaphoreType.DMA
    v = pltpu.VMEM
    gather_sems = [dma((CHIPS, 2)), dma((CHIPS,)), dma((CHIPS, 2)), dma((CHIPS, 2)), dma((CHIPS,))]
    scratch = [
        v((9, 2, 2, ROWS, COLS), BF16),
        v((64, 96, FFB), BF16),
        v((256, 2048), BF16),
        v((ROWS, COLS), BF16),
        v((ROWS, 512), BF16),
        v((ROWS, 512), BF16),
        v((2, ROWS, 128), F32),
        v((2, ROWS, 128), F32),
        v((2, ROWS, 128), F32),
        v((ROWS, 512), F32),
        v((3, ROWS, 512), BF16),
        v((3, ROWS, 512), BF16),
        v((2, 3, ROWS, COLS), BF16),
        v((2, 3, ROWS, COLS), BF16),
        v((NX, ROWS, 512), BF16),
        v((ROWS, COLS), BF16),
        v((ROWS, COLS), BF16),
        v((2, ROWS, COLS), F32),
        v((ROWS, FFB), BF16),
        dma((6,)), dma((9,)), dma((9,)), dma((5,)), dma((3,)), dma((9,)),
        *gather_sems,
        dma((4, 3)), dma((4, 3)), dma((4, 3)), dma((4, 3)), dma((2, 2, 3)), dma((2, 2, 3)),
        dma((2, 4)), dma((2, 2)),
    ]
    return pl.pallas_call(
        kernel,
        out_shape=jax.ShapeDtypeStruct((ROWS, COLS), BF16),
        in_specs=[vmem, vmem, smem, smem, vmem] + [hbm] * 6,
        out_specs=vmem,
        scratch_shapes=scratch,
        compiler_params=pltpu.CompilerParams(
            collective_id=0, has_side_effects=True, vmem_limit_bytes=60 * 1024 * 1024
        ),
        name="layer",
    )(
        queries, residual_in, bias_table, buckets, norm_gain.reshape(1, -1),
        keys, values, out_weight, gate_weight, up_weight, down_weight_t,
    )


def solution(mesh):
    return jax.shard_map(
        shards,
        mesh=mesh,
        in_specs=(
            P("seq", "tp"),
            P("seq", "tp"),
            P("seq", "tp"),
            P("seq", "tp"),
            P("tp", None),
            P("seq", None),
            P("tp", None),
            P("seq", "tp"),
            P("seq", "tp"),
            P("seq", "tp"),
            P(),
        ),
        out_specs=P("seq", "tp"),
        check_vma=False,
    )
```
